128 devices in a mesh: gx: 16 (over x, y), gy: 8 (over z, core).
Axes of the slice: x: 4, y: 4, z: 4, core: 2. Of those that a mesh axis runs over, the one named last changes fastest.
Arguments:
- plume_field: bfloat16 [2, 20, 128, 128, 16, 128], P(None, None, 'gx', 'gy'), may hold values from -6 to 6
- mode_weights: bfloat16 [24, 20, 20, 16, 2, 288], P('gy', None, None, 'gx'), may hold values from -1 to 1
Outputs:
- spectral_mix: float32 [2, 24, 20, 16, 2, 288], P(None, 'gy', None, 'gx')
The draws below stay inside these ranges and needn't reach their ends.
All inputs are finite; a program needn't handle non-finite values.
Results may differ from the reference program's by a relative error of at most 0.003.
Values sent between devices are 32-bit elements; how exact they have to be, the bound alone decides.
A program may use at most 192 MiB of HBM per device.

```python
import math
import jax
import jax.numpy as jnp
from jax import lax

BATCH = 2
CHANNELS = 20
GRID_X = 128
GRID_Y = 128
GRID_Z = 128
STEPS_T = 16
MODES_X = 24
MODES_Y = 24
MODES_Z = 24
MODES_T = 8
HALF_Z = 12
GROUPS = 16


def shard_levels(rng, dims, shards, least, largest):
    factor_of, own = 1.0, jax.random.fold_in(rng, 6)
    for axis_at, blocks in shards:
        draws = jnp.exp(jax.random.uniform(jax.random.fold_in(own, axis_at), (blocks,), jnp.float32, least / len(shards), largest / len(shards)))
        factor_of = factor_of * jnp.repeat(draws, dims[axis_at] // blocks).reshape([-1 if axis == axis_at else 1 for axis in range(len(dims))])
    return factor_of


def bell_draw(stream_key, dims, deviation, reach, pieces=(), held_as=jnp.bfloat16):
    values = deviation * jax.random.normal(stream_key, dims, jnp.float32)
    if pieces:
        values = values * shard_levels(stream_key, dims, pieces, -0.22, 0.18)
    return jnp.clip(values, -reach, reach).astype(held_as)


def setup_inputs(seed: int = 0) -> dict:
    keys = jax.random.split(jax.random.key(seed), 3)
    return {
        "plume_field": bell_draw(keys[0], (BATCH, CHANNELS, GRID_X, GRID_Y, STEPS_T, GRID_Z), 1.0, 6.0, ((2, 16), (3, 8))),
        "mode_weights": bell_draw(keys[1], (MODES_X, CHANNELS, CHANNELS, GROUPS, 2, HALF_Z * MODES_Y), (2 * CHANNELS) ** -0.5, 1.0, ((0, 8), (3, 16))),
    }


def kept_modes(kept_count, axis_length):
    position = jnp.arange(kept_count, dtype=jnp.int32)
    return jnp.where(position < kept_count // 2, position, axis_length - kept_count + position)

def plane_table():
    moments = jnp.arange(STEPS_T, dtype=jnp.int32)
    depths = jnp.arange(GRID_Z, dtype=jnp.int32)
    time_freq = jnp.arange(MODES_T, dtype=jnp.int32)
    depth_freq = kept_modes(MODES_Z, GRID_Z).reshape(2, HALF_Z)
    phase_index = (time_freq[None, None, :, None, None] * moments[:, None, None, None, None] * (GRID_Z // STEPS_T) + depth_freq[None, None, None, :, :] * depths[None, :, None, None, None]) % GRID_Z
    phases = 2.0 * math.pi / GRID_Z * phase_index.astype(jnp.float32)
    factor = 1.0 / math.sqrt(STEPS_T * GRID_Z)
    twiddle = jnp.stack([factor * jnp.cos(phases), -factor * jnp.sin(phases)], axis=4)
    return twiddle.reshape(STEPS_T * GRID_Z, 2 * MODES_T * MODES_Z).astype(jnp.bfloat16)

def line_table(kept_count, axis_length, positions):
    frequency = kept_modes(kept_count, axis_length)
    phase_index = positions[:, None] * frequency[None, :] % axis_length
    phases = 2.0 * math.pi / axis_length * phase_index.astype(jnp.float32)
    factor = 1.0 / math.sqrt(axis_length)
    cosines = factor * jnp.cos(phases)
    sines = factor * jnp.sin(phases)
    upper_row = jnp.stack([cosines, -sines], axis=1)
    lower_row = jnp.stack([sines, cosines], axis=1)
    return jnp.stack([upper_row, lower_row], axis=1)

def mix_modes(modes, mode_weights):
    highest = lax.Precision.HIGHEST
    real_part = modes[:, :, :, :, 0]
    imag_part = modes[:, :, :, :, 1]
    weight_re = mode_weights[:, :, :, :, 0].astype(jnp.float32)
    weight_im = mode_weights[:, :, :, :, 1].astype(jnp.float32)
    mixed_re = jnp.einsum('kbcgz,kcogz->bkogz', real_part, weight_re, precision=highest) - jnp.einsum('kbcgz,kcogz->bkogz', imag_part, weight_im, precision=highest)
    mixed_im = jnp.einsum('kbcgz,kcogz->bkogz', real_part, weight_im, precision=highest) + jnp.einsum('kbcgz,kcogz->bkogz', imag_part, weight_re, precision=highest)
    return jnp.stack([mixed_re, mixed_im], axis=4)

def reference(plume_field, mode_weights):
    highest = lax.Precision.HIGHEST
    twiddle = plane_table()
    columns = 2 * MODES_T * MODES_Z
    slab_rows = math.gcd(GRID_X, 8)

    def transform_slab(first_row):
        portion = lax.dynamic_slice_in_dim(plume_field, first_row, slab_rows, 2)
        flat = portion.reshape(-1, STEPS_T * GRID_Z)
        product = jnp.dot(flat, twiddle, preferred_element_type=jnp.float32)
        return product.reshape(BATCH, CHANNELS, slab_rows, GRID_Y, columns)
    starts = jnp.arange(GRID_X // slab_rows, dtype=jnp.int32) * slab_rows
    slabs = lax.map(transform_slab, starts)
    spectrum = jnp.moveaxis(slabs, 0, 2).reshape(BATCH, CHANNELS, GRID_X, GRID_Y, GROUPS, 2, HALF_Z)
    first_twiddle = line_table(MODES_X, GRID_X, jnp.arange(GRID_X, dtype=jnp.int32))
    x_modes = jnp.einsum('bcxygrz,xrsk->bckygsz', spectrum, first_twiddle, precision=highest)
    second_twiddle = line_table(MODES_Y, GRID_Y, jnp.arange(GRID_Y, dtype=jnp.int32))
    y_modes = jnp.einsum('bckygrz,yrsl->kbcgszl', x_modes, second_twiddle, precision=highest)
    y_modes = y_modes.reshape(MODES_X, BATCH, CHANNELS, GROUPS, 2, HALF_Z * MODES_Y)
    return mix_modes(y_modes, mode_weights)
```

```python
import math

import jax
import jax.numpy as jnp
from jax import lax
from jax.sharding import PartitionSpec as P

GRID_X = 128
GRID_Y = 128
GRID_Z = 128
STEPS_T = 16
MODES_X = 24
MODES_Y = 24
MODES_Z = 24
MODES_T = 8
HALF_Z = 12


def kept_modes(kept_count, axis_length):
    position = jnp.arange(kept_count, dtype=jnp.int32)
    return jnp.where(position < kept_count // 2, position, axis_length - kept_count + position)


def plane_table():
    moments = jnp.arange(STEPS_T, dtype=jnp.int32)
    depths = jnp.arange(GRID_Z, dtype=jnp.int32)
    time_freq = jnp.arange(MODES_T, dtype=jnp.int32)
    depth_freq = kept_modes(MODES_Z, GRID_Z).reshape(2, HALF_Z)
    phase_index = (
        time_freq[None, None, :, None, None]
        * moments[:, None, None, None, None]
        * (GRID_Z // STEPS_T)
        + depth_freq[None, None, None, :, :] * depths[None, :, None, None, None]
    ) % GRID_Z
    phases = 2.0 * math.pi / GRID_Z * phase_index.astype(jnp.float32)
    factor = 1.0 / math.sqrt(STEPS_T * GRID_Z)
    twiddle = jnp.stack([factor * jnp.cos(phases), -factor * jnp.sin(phases)], axis=4)
    return twiddle.reshape(STEPS_T, GRID_Z, 2 * MODES_T * MODES_Z).astype(jnp.bfloat16)


def line_matrix(kept_count, axis_length):
    frequency = kept_modes(kept_count, axis_length)
    positions = jnp.arange(axis_length, dtype=jnp.int32)
    phase_index = frequency[:, None] * positions[None, :] % axis_length
    phases = 2.0 * math.pi / axis_length * phase_index.astype(jnp.float32)
    factor = 1.0 / math.sqrt(axis_length)
    cosines = factor * jnp.cos(phases)
    sines = factor * jnp.sin(phases)
    upper = jnp.stack([cosines, sines], axis=1)
    lower = jnp.stack([-sines, cosines], axis=1)
    return jnp.stack([upper, lower], axis=0)


def local(plume_field, mode_weights):
    highest = lax.Precision.HIGHEST
    samples, channels, rows_x, rows_y = plume_field.shape[:4]
    parts_x = GRID_X // rows_x
    parts_y = GRID_Y // rows_y
    groups = 2 * MODES_T
    per_group = 2 * HALF_Z
    kept_here = MODES_X // parts_y

    twiddle = plane_table()
    spectrum = lax.dot_general(
        twiddle, plume_field, (((0, 1), (4, 5)), ((), ())), preferred_element_type=jnp.float32
    )
    spectrum = spectrum.reshape(groups, per_group, samples * channels * rows_x * rows_y)
    moved = lax.all_to_all(spectrum, "gx", 0, 0, tiled=False)
    moved = moved.reshape(parts_x, 2, HALF_Z, samples, channels, rows_x, rows_y)

    first = line_matrix(MODES_X, GRID_X).reshape(2, parts_y, kept_here, 2, parts_x, rows_x)
    after_x = jnp.einsum("sKqrip,irjbcpy->Kysqjbc", first, moved, precision=highest)
    after_x = after_x.reshape(parts_y, rows_y, -1)
    gathered = lax.all_to_all(after_x, "gy", 0, 0, tiled=False)
    gathered = gathered.reshape(GRID_Y, 2, kept_here, HALF_Z, samples, channels)

    second = line_matrix(MODES_Y, GRID_Y)
    after_y = jnp.einsum("tlsy,yskjbc->kbctjl", second, gathered, precision=highest)
    after_y = after_y.reshape(kept_here, samples, channels, 2, HALF_Z * MODES_Y)

    real_part = after_y[:, :, :, None, 0]
    imag_part = after_y[:, :, :, None, 1]
    weight_re = mode_weights[:, None, :, :, 0, 0].astype(jnp.float32)
    weight_im = mode_weights[:, None, :, :, 0, 1].astype(jnp.float32)
    mixed_re = jnp.sum(real_part * weight_re - imag_part * weight_im, axis=2)
    mixed_im = jnp.sum(real_part * weight_im + imag_part * weight_re, axis=2)
    mixed = jnp.stack([mixed_re, mixed_im], axis=3)[:, :, :, None]
    return jnp.swapaxes(mixed, 0, 1)


def solution(mesh):
    return jax.shard_map(
        local,
        mesh=mesh,
        in_specs=(P(None, None, "gx", "gy", None, None), P("gy", None, None, "gx", None, None)),
        out_specs=P(None, "gy", None, "gx", None, None),
        check_vma=False,
    )
```

```python
import math

import jax
import jax.numpy as jnp
from jax import lax
from jax.sharding import PartitionSpec as P

GRID_X = 128
GRID_Y = 128
GRID_Z = 128
STEPS_T = 16
MODES_X = 24
MODES_Y = 24
MODES_Z = 24
MODES_T = 8
HALF_Z = 12


def kept_modes(kept_count, axis_length):
    position = jnp.arange(kept_count, dtype=jnp.int32)
    return jnp.where(position < kept_count // 2, position, axis_length - kept_count + position)


def plane_table():
    moments = jnp.arange(STEPS_T, dtype=jnp.int32)
    depths = jnp.arange(GRID_Z, dtype=jnp.int32)
    time_freq = jnp.arange(MODES_T, dtype=jnp.int32)
    depth_freq = kept_modes(MODES_Z, GRID_Z).reshape(2, HALF_Z)
    phase_index = (
        time_freq[None, None, :, None, None]
        * moments[:, None, None, None, None]
        * (GRID_Z // STEPS_T)
        + depth_freq[None, None, None, :, :] * depths[None, :, None, None, None]
    ) % GRID_Z
    phases = 2.0 * math.pi / GRID_Z * phase_index.astype(jnp.float32)
    factor = 1.0 / math.sqrt(STEPS_T * GRID_Z)
    twiddle = jnp.stack([factor * jnp.cos(phases), -factor * jnp.sin(phases)], axis=4)
    return twiddle.reshape(STEPS_T, GRID_Z, 2 * MODES_T * MODES_Z).astype(jnp.bfloat16)


def line_parts(kept_count, axis_length):
    frequency = kept_modes(kept_count, axis_length)
    positions = jnp.arange(axis_length, dtype=jnp.int32)
    phase_index = frequency[:, None] * positions[None, :] % axis_length
    phases = 2.0 * math.pi / axis_length * phase_index.astype(jnp.float32)
    factor = 1.0 / math.sqrt(axis_length)
    return factor * jnp.cos(phases), factor * jnp.sin(phases)


def line_matrix(kept_count, axis_length):
    frequency = kept_modes(kept_count, axis_length)
    positions = jnp.arange(axis_length, dtype=jnp.int32)
    phase_index = frequency[:, None] * positions[None, :] % axis_length
    phases = 2.0 * math.pi / axis_length * phase_index.astype(jnp.float32)
    factor = 1.0 / math.sqrt(axis_length)
    cosines = factor * jnp.cos(phases)
    sines = factor * jnp.sin(phases)
    upper = jnp.stack([cosines, sines], axis=1)
    lower = jnp.stack([-sines, cosines], axis=1)
    return jnp.stack([upper, lower], axis=0)


def local(plume_field, mode_weights):
    high = lax.Precision.HIGH
    samples, channels, rows_x, rows_y = plume_field.shape[:4]
    parts_x = GRID_X // rows_x
    parts_y = GRID_Y // rows_y
    groups = 2 * MODES_T
    per_group = 2 * HALF_Z
    kept_here = MODES_X // parts_y
    lanes = rows_x * rows_y
    pairs = samples * channels

    twiddle = plane_table()
    field = plume_field.reshape(pairs, lanes, STEPS_T, GRID_Z)
    spectrum = jnp.einsum("tzn,Bxtz->Bnx", twiddle, field, preferred_element_type=jnp.float32)
    spectrum = spectrum.reshape(pairs, groups, per_group, lanes)
    moved = lax.all_to_all(spectrum, "gx", 1, 1, tiled=False)

    cosines, sines = line_parts(MODES_X, GRID_X)
    parts = jnp.stack([cosines, sines], axis=0).reshape(2, parts_y, kept_here, parts_x, rows_x)
    eye_y = jnp.eye(rows_y, dtype=jnp.float32)
    kron = parts[:, :, :, None, :, :, None] * eye_y[:, None, None, :]
    kron = jnp.transpose(kron, (4, 5, 6, 0, 1, 2, 3))
    kron = kron.reshape(parts_x, lanes, 2, parts_y, kept_here * rows_y)
    both = lax.dot_general(moved, kron, (((1, 3), (0, 1)), ((), ())), precision=high)
    both = both.reshape(pairs, 2, HALF_Z, 2, parts_y, kept_here * rows_y)
    out_re = both[:, 0, :, 0] + both[:, 1, :, 1]
    out_im = both[:, 1, :, 0] - both[:, 0, :, 1]
    after_x = jnp.stack([out_re, out_im], axis=0)
    after_x = jnp.transpose(after_x, (3, 0, 4, 2, 1))
    after_x = after_x.reshape(parts_y, 2 * kept_here * rows_y, HALF_Z * pairs)
    gathered = lax.all_to_all(after_x, "gy", 0, 0, tiled=False)
    gathered = gathered.reshape(parts_y, 2, kept_here, rows_y, HALF_Z * pairs)

    second = line_matrix(MODES_Y, GRID_Y).reshape(2, MODES_Y, 2, parts_y, rows_y)
    after_y = lax.dot_general(second, gathered, (((2, 3, 4), (1, 0, 3)), ((), ())), precision=high)
    after_y = after_y.reshape(2, MODES_Y, kept_here, HALF_Z, samples, channels)
    after_y = jnp.transpose(after_y, (2, 4, 5, 0, 3, 1))
    after_y = after_y.reshape(kept_here, samples, channels, 2, HALF_Z * MODES_Y)

    real_part = after_y[:, :, :, None, 0]
    imag_part = after_y[:, :, :, None, 1]
    weight_re = mode_weights[:, None, :, :, 0, 0].astype(jnp.float32)
    weight_im = mode_weights[:, None, :, :, 0, 1].astype(jnp.float32)
    mixed_re = jnp.sum(real_part * weight_re - imag_part * weight_im, axis=2)
    mixed_im = jnp.sum(real_part * weight_im + imag_part * weight_re, axis=2)
    mixed = jnp.stack([mixed_re, mixed_im], axis=3)[:, :, :, None]
    return jnp.swapaxes(mixed, 0, 1)


def solution(mesh):
    return jax.shard_map(
        local,
        mesh=mesh,
        in_specs=(P(None, None, "gx", "gy", None, None), P("gy", None, None, "gx", None, None)),
        out_specs=P(None, "gy", None, "gx", None, None),
        check_vma=False,
    )
```

```python
import math

import jax
import jax.numpy as jnp
from jax import lax
from jax.sharding import PartitionSpec as P

GRID_X = 128
GRID_Y = 128
GRID_Z = 128
STEPS_T = 16
MODES_X = 24
MODES_Y = 24
MODES_Z = 24
MODES_T = 8
HALF_Z = 12


def kept_modes(kept_count, axis_length):
    position = jnp.arange(kept_count, dtype=jnp.int32)
    return jnp.where(position < kept_count // 2, position, axis_length - kept_count + position)


def plane_table():
    moments = jnp.arange(STEPS_T, dtype=jnp.int32)
    depths = jnp.arange(GRID_Z, dtype=jnp.int32)
    time_freq = jnp.arange(MODES_T, dtype=jnp.int32)
    depth_freq = kept_modes(MODES_Z, GRID_Z).reshape(2, HALF_Z)
    phase_index = (
        time_freq[None, None, :, None, None]
        * moments[:, None, None, None, None]
        * (GRID_Z // STEPS_T)
        + depth_freq[None, None, None, :, :] * depths[None, :, None, None, None]
    ) % GRID_Z
    phases = 2.0 * math.pi / GRID_Z * phase_index.astype(jnp.float32)
    factor = 1.0 / math.sqrt(STEPS_T * GRID_Z)
    twiddle = jnp.stack([factor * jnp.cos(phases), -factor * jnp.sin(phases)], axis=4)
    return twiddle.reshape(STEPS_T, GRID_Z, 2 * MODES_T * MODES_Z).astype(jnp.bfloat16)


def line_parts(kept_count, axis_length):
    frequency = kept_modes(kept_count, axis_length)
    positions = jnp.arange(axis_length, dtype=jnp.int32)
    phase_index = frequency[:, None] * positions[None, :] % axis_length
    phases = 2.0 * math.pi / axis_length * phase_index.astype(jnp.float32)
    factor = 1.0 / math.sqrt(axis_length)
    return factor * jnp.cos(phases), factor * jnp.sin(phases)


def line_matrix(kept_count, axis_length):
    frequency = kept_modes(kept_count, axis_length)
    positions = jnp.arange(axis_length, dtype=jnp.int32)
    phase_index = frequency[:, None] * positions[None, :] % axis_length
    phases = 2.0 * math.pi / axis_length * phase_index.astype(jnp.float32)
    factor = 1.0 / math.sqrt(axis_length)
    cosines = factor * jnp.cos(phases)
    sines = factor * jnp.sin(phases)
    upper = jnp.stack([cosines, sines], axis=1)
    lower = jnp.stack([-sines, cosines], axis=1)
    return jnp.stack([upper, lower], axis=0)


def plane_table_fast():
    moments = jnp.arange(STEPS_T, dtype=jnp.int32)
    depths = jnp.arange(GRID_Z, dtype=jnp.int32)
    time_freq = jnp.arange(MODES_T, dtype=jnp.int32)
    depth_freq = kept_modes(MODES_Z, GRID_Z)
    step = 2.0 * math.pi / GRID_Z
    time_phase = step * ((moments[:, None] * time_freq[None, :] * (GRID_Z // STEPS_T)) % GRID_Z).astype(jnp.float32)
    depth_phase = step * ((depths[:, None] * depth_freq[None, :]) % GRID_Z).astype(jnp.float32)
    factor = 1.0 / math.sqrt(STEPS_T * GRID_Z)
    ct = (factor * jnp.cos(time_phase))[:, None, :, None]
    st = (factor * jnp.sin(time_phase))[:, None, :, None]
    cz = jnp.cos(depth_phase)[None, :, None, :]
    sz = jnp.sin(depth_phase)[None, :, None, :]
    cos_part = ct * cz - st * sz
    sin_part = st * cz + ct * sz
    twiddle = jnp.stack([cos_part.reshape(STEPS_T, GRID_Z, MODES_T, 2, HALF_Z),
                         -sin_part.reshape(STEPS_T, GRID_Z, MODES_T, 2, HALF_Z)], axis=4)
    return twiddle.reshape(STEPS_T, GRID_Z, 2 * MODES_T * MODES_Z).astype(jnp.bfloat16)


def one_sample(field, mode_weights, twiddle, kron, second):
    high = lax.Precision.HIGH
    pairs, lanes = field.shape[:2]
    groups = 2 * MODES_T
    per_group = 2 * HALF_Z
    parts_y = second.shape[0]
    rows_y = second.shape[1] // 2
    kept_here = MODES_X // parts_y

    spectrum = jnp.einsum("tzn,Bxtz->Bnx", twiddle, field, preferred_element_type=jnp.float32)
    spectrum = spectrum.reshape(pairs, groups, per_group, lanes)
    moved = lax.all_to_all(spectrum, "gx", 1, 1, tiled=False)

    both = lax.dot_general(moved, kron, (((1, 3), (2, 4)), ((), ())), precision=high)
    both = both.reshape(pairs, 2, HALF_Z, 2, parts_y, kept_here, rows_y)
    out_re = both[:, 0, :, 0] + both[:, 1, :, 1]
    out_im = both[:, 1, :, 0] - both[:, 0, :, 1]
    after_x = jnp.stack([out_re, out_im], axis=0)
    after_x = jnp.transpose(after_x, (3, 4, 0, 5, 2, 1))
    after_x = after_x.reshape(parts_y, kept_here * 2 * rows_y, HALF_Z * pairs)
    gathered = lax.all_to_all(after_x, "gy", 0, 0, tiled=False)
    gathered = gathered.reshape(parts_y, kept_here, 2 * rows_y, HALF_Z * pairs)

    after_y = lax.dot_general(gathered, second, (((0, 2), (0, 1)), ((1,), (2,))), precision=high)
    after_y = after_y.reshape(kept_here, HALF_Z, pairs, 2, MODES_Y)
    after_y = jnp.transpose(after_y, (0, 2, 3, 1, 4))
    after_y = after_y.reshape(kept_here, pairs, 2, HALF_Z * MODES_Y)

    real_part = after_y[:, :, None, 0]
    imag_part = after_y[:, :, None, 1]
    weight_re = mode_weights[:, :, :, 0, 0].astype(jnp.float32)
    weight_im = mode_weights[:, :, :, 0, 1].astype(jnp.float32)
    mixed_re = jnp.sum(real_part * weight_re - imag_part * weight_im, axis=1)
    mixed_im = jnp.sum(real_part * weight_im + imag_part * weight_re, axis=1)
    return jnp.stack([mixed_re, mixed_im], axis=2)[:, :, None]


def local(plume_field, mode_weights):
    samples, channels, rows_x, rows_y = plume_field.shape[:4]
    parts_x = GRID_X // rows_x
    parts_y = GRID_Y // rows_y
    kept_here = MODES_X // parts_y
    lanes = rows_x * rows_y

    twiddle = plane_table_fast()

    cosines, sines = line_parts(MODES_X, GRID_X)
    parts = jnp.stack([cosines, sines], axis=0).reshape(2, parts_y, kept_here, parts_x, rows_x)
    parts = jnp.transpose(parts, (0, 1, 3, 2, 4))
    eye_y = jnp.eye(rows_y, dtype=jnp.float32)
    kron = parts[:, :, :, :, None, :, None] * eye_y[:, None, :]
    kron = kron.reshape(2, parts_y, parts_x, kept_here * rows_y, lanes)

    second = line_matrix(MODES_Y, GRID_Y).reshape(2, MODES_Y, 2, parts_y, rows_y)
    second = jnp.transpose(second, (3, 2, 4, 0, 1)).reshape(parts_y, 2 * rows_y, 1, 2 * MODES_Y)
    second = jnp.broadcast_to(second, (parts_y, 2 * rows_y, kept_here, 2 * MODES_Y))

    outs = []
    for sample in range(samples):
        field = plume_field[sample].reshape(channels, lanes, STEPS_T, GRID_Z)
        outs.append(one_sample(field, mode_weights, twiddle, kron, second))
    return jnp.stack(outs, axis=0)


def solution(mesh):
    return jax.shard_map(
        local,
        mesh=mesh,
        in_specs=(P(None, None, "gx", "gy", None, None), P("gy", None, None, "gx", None, None)),
        out_specs=P(None, "gy", None, "gx", None, None),
        check_vma=False,
    )
```

```python
import math

import jax
import jax.numpy as jnp
from jax import lax
from jax.sharding import PartitionSpec as P

GRID_X = 128
GRID_Y = 128
GRID_Z = 128
STEPS_T = 16
MODES_X = 24
MODES_Y = 24
MODES_Z = 24
MODES_T = 8
HALF_Z = 12


def kept_modes(kept_count, axis_length):
    position = jnp.arange(kept_count, dtype=jnp.int32)
    return jnp.where(position < kept_count // 2, position, axis_length - kept_count + position)


def plane_table():
    moments = jnp.arange(STEPS_T, dtype=jnp.int32)
    depths = jnp.arange(GRID_Z, dtype=jnp.int32)
    time_freq = jnp.arange(MODES_T, dtype=jnp.int32)
    depth_freq = kept_modes(MODES_Z, GRID_Z).reshape(2, HALF_Z)
    phase_index = (
        time_freq[None, None, :, None, None]
        * moments[:, None, None, None, None]
        * (GRID_Z // STEPS_T)
        + depth_freq[None, None, None, :, :] * depths[None, :, None, None, None]
    ) % GRID_Z
    phases = 2.0 * math.pi / GRID_Z * phase_index.astype(jnp.float32)
    factor = 1.0 / math.sqrt(STEPS_T * GRID_Z)
    twiddle = jnp.stack([factor * jnp.cos(phases), -factor * jnp.sin(phases)], axis=4)
    return twiddle.reshape(STEPS_T, GRID_Z, 2 * MODES_T * MODES_Z).astype(jnp.bfloat16)


def line_parts(kept_count, axis_length):
    frequency = kept_modes(kept_count, axis_length)
    positions = jnp.arange(axis_length, dtype=jnp.int32)
    phase_index = frequency[:, None] * positions[None, :] % axis_length
    phases = 2.0 * math.pi / axis_length * phase_index.astype(jnp.float32)
    factor = 1.0 / math.sqrt(axis_length)
    return factor * jnp.cos(phases), factor * jnp.sin(phases)


def line_matrix(kept_count, axis_length):
    frequency = kept_modes(kept_count, axis_length)
    positions = jnp.arange(axis_length, dtype=jnp.int32)
    phase_index = frequency[:, None] * positions[None, :] % axis_length
    phases = 2.0 * math.pi / axis_length * phase_index.astype(jnp.float32)
    factor = 1.0 / math.sqrt(axis_length)
    cosines = factor * jnp.cos(phases)
    sines = factor * jnp.sin(phases)
    upper = jnp.stack([cosines, sines], axis=1)
    lower = jnp.stack([-sines, cosines], axis=1)
    return jnp.stack([upper, lower], axis=0)


def local(plume_field, mode_weights):
    high = lax.Precision.HIGH
    samples, channels, rows_x, rows_y = plume_field.shape[:4]
    parts_x = GRID_X // rows_x
    parts_y = GRID_Y // rows_y
    groups = 2 * MODES_T
    per_group = 2 * HALF_Z
    kept_here = MODES_X // parts_y
    lanes = rows_x * rows_y
    pairs = samples * channels

    twiddle = plane_table()
    field = plume_field.reshape(pairs, lanes, STEPS_T, GRID_Z)
    spectrum = jnp.einsum("tzn,Bxtz->Bnx", twiddle, field, preferred_element_type=jnp.float32)
    spectrum = spectrum.reshape(pairs, groups, per_group, lanes)
    moved = lax.all_to_all(spectrum, "gx", 1, 1, tiled=False)

    cosines, sines = line_parts(MODES_X, GRID_X)
    parts = jnp.stack([cosines, sines], axis=0).reshape(2, parts_y, kept_here, parts_x, rows_x)
    eye_y = jnp.eye(rows_y, dtype=jnp.float32)
    kron = parts[:, :, :, None, :, :, None] * eye_y[:, None, None, :]
    kron = jnp.transpose(kron, (4, 5, 6, 0, 1, 2, 3))
    kron = kron.reshape(parts_x, lanes, 2, parts_y, kept_here * rows_y)
    both = lax.dot_general(moved, kron, (((1, 3), (0, 1)), ((), ())), precision=high)
    both = both.reshape(pairs, 2, HALF_Z, 2, parts_y, kept_here * rows_y)
    out_re = both[:, 0, :, 0] + both[:, 1, :, 1]
    out_im = both[:, 1, :, 0] - both[:, 0, :, 1]
    after_x = jnp.stack([out_re, out_im], axis=0)
    after_x = after_x.reshape(2, pairs, HALF_Z, parts_y, kept_here, rows_y)
    after_x = jnp.transpose(after_x, (3, 4, 0, 5, 2, 1))
    after_x = after_x.reshape(parts_y, kept_here * 2 * rows_y, HALF_Z * pairs)
    gathered = lax.all_to_all(after_x, "gy", 0, 0, tiled=False)
    gathered = gathered.reshape(parts_y, kept_here, 2 * rows_y, HALF_Z * pairs)

    second = line_matrix(MODES_Y, GRID_Y).reshape(2, MODES_Y, 2, parts_y, rows_y)
    second = jnp.transpose(second, (3, 2, 4, 0, 1)).reshape(parts_y, 2 * rows_y, 1, 2 * MODES_Y)
    second = jnp.broadcast_to(second, (parts_y, 2 * rows_y, kept_here, 2 * MODES_Y))
    after_y = lax.dot_general(gathered, second, (((0, 2), (0, 1)), ((1,), (2,))), precision=high)
    after_y = after_y.reshape(kept_here, HALF_Z, samples, channels, 2, MODES_Y)
    after_y = jnp.transpose(after_y, (0, 2, 3, 4, 1, 5))
    after_y = after_y.reshape(kept_here, samples, channels, 2, HALF_Z * MODES_Y)


    real_part = after_y[:, :, :, None, 0]
    imag_part = after_y[:, :, :, None, 1]
    weight_re = mode_weights[:, None, :, :, 0, 0].astype(jnp.float32)
    weight_im = mode_weights[:, None, :, :, 0, 1].astype(jnp.float32)
    mixed_re = jnp.sum(real_part * weight_re - imag_part * weight_im, axis=2)
    mixed_im = jnp.sum(real_part * weight_im + imag_part * weight_re, axis=2)
    mixed = jnp.stack([mixed_re, mixed_im], axis=3)[:, :, :, None]
    return jnp.swapaxes(mixed, 0, 1)


def solution(mesh):
    return jax.shard_map(
        local,
        mesh=mesh,
        in_specs=(P(None, None, "gx", "gy", None, None), P("gy", None, None, "gx", None, None)),
        out_specs=P(None, "gy", None, "gx", None, None),
        check_vma=False,
    )
```

```python
import math

import jax
import jax.numpy as jnp
from jax import lax
from jax.sharding import PartitionSpec as P

GRID_X = 128
GRID_Y = 128
GRID_Z = 128
STEPS_T = 16
MODES_X = 24
MODES_Y = 24
MODES_Z = 24
MODES_T = 8
HALF_Z = 12


def kept_modes(kept_count, axis_length):
    position = jnp.arange(kept_count, dtype=jnp.int32)
    return jnp.where(position < kept_count // 2, position, axis_length - kept_count + position)


def plane_table():
    moments = jnp.arange(STEPS_T, dtype=jnp.int32)
    depths = jnp.arange(GRID_Z, dtype=jnp.int32)
    time_freq = jnp.arange(MODES_T, dtype=jnp.int32)
    depth_freq = kept_modes(MODES_Z, GRID_Z).reshape(2, HALF_Z)
    phase_index = (
        time_freq[None, None, :, None, None]
        * moments[:, None, None, None, None]
        * (GRID_Z // STEPS_T)
        + depth_freq[None, None, None, :, :] * depths[None, :, None, None, None]
    ) % GRID_Z
    phases = 2.0 * math.pi / GRID_Z * phase_index.astype(jnp.float32)
    factor = 1.0 / math.sqrt(STEPS_T * GRID_Z)
    twiddle = jnp.stack([factor * jnp.cos(phases), -factor * jnp.sin(phases)], axis=4)
    return twiddle.reshape(STEPS_T, GRID_Z, 2 * MODES_T * MODES_Z).astype(jnp.bfloat16)


def line_parts(kept_count, axis_length):
    frequency = kept_modes(kept_count, axis_length)
    positions = jnp.arange(axis_length, dtype=jnp.int32)
    phase_index = frequency[:, None] * positions[None, :] % axis_length
    phases = 2.0 * math.pi / axis_length * phase_index.astype(jnp.float32)
    factor = 1.0 / math.sqrt(axis_length)
    return factor * jnp.cos(phases), factor * jnp.sin(phases)


def line_matrix(kept_count, axis_length):
    frequency = kept_modes(kept_count, axis_length)
    positions = jnp.arange(axis_length, dtype=jnp.int32)
    phase_index = frequency[:, None] * positions[None, :] % axis_length
    phases = 2.0 * math.pi / axis_length * phase_index.astype(jnp.float32)
    factor = 1.0 / math.sqrt(axis_length)
    cosines = factor * jnp.cos(phases)
    sines = factor * jnp.sin(phases)
    upper = jnp.stack([cosines, sines], axis=1)
    lower = jnp.stack([-sines, cosines], axis=1)
    return jnp.stack([upper, lower], axis=0)


def one_sample(moved, mode_weights, kron, second):
    high = lax.Precision.HIGH
    pairs, parts_x, _, lanes = moved.shape
    parts_y = second.shape[0]
    rows_y = second.shape[1] // 2
    kept_here = MODES_X // parts_y

    both = lax.dot_general(moved, kron, (((1, 3), (0, 1)), ((), ())), precision=high)
    both = both.reshape(pairs, 2, HALF_Z, 2, parts_y, kept_here * rows_y)
    out_re = both[:, 0, :, 0] + both[:, 1, :, 1]
    out_im = both[:, 1, :, 0] - both[:, 0, :, 1]
    after_x = jnp.stack([out_re, out_im], axis=0)
    after_x = after_x.reshape(2, pairs, HALF_Z, parts_y, kept_here, rows_y)
    after_x = jnp.transpose(after_x, (3, 4, 0, 5, 2, 1))
    after_x = after_x.reshape(parts_y, kept_here * 2 * rows_y, HALF_Z * pairs)
    gathered = lax.all_to_all(after_x, "gy", 0, 0, tiled=False)
    gathered = gathered.reshape(parts_y, kept_here, 2 * rows_y, HALF_Z * pairs)

    after_y = lax.dot_general(gathered, second, (((0, 2), (0, 1)), ((1,), (2,))), precision=high)
    after_y = after_y.reshape(kept_here, HALF_Z, pairs, 2, MODES_Y)
    after_y = jnp.transpose(after_y, (0, 2, 3, 1, 4))
    after_y = after_y.reshape(kept_here, pairs, 2, HALF_Z * MODES_Y)

    real_part = after_y[:, :, None, 0]
    imag_part = after_y[:, :, None, 1]
    weight_re = mode_weights[:, :, :, 0, 0].astype(jnp.float32)
    weight_im = mode_weights[:, :, :, 0, 1].astype(jnp.float32)
    mixed_re = jnp.sum(real_part * weight_re - imag_part * weight_im, axis=1)
    mixed_im = jnp.sum(real_part * weight_im + imag_part * weight_re, axis=1)
    return jnp.stack([mixed_re, mixed_im], axis=2)[:, :, None]


def local(plume_field, mode_weights):
    samples, channels, rows_x, rows_y = plume_field.shape[:4]
    parts_x = GRID_X // rows_x
    parts_y = GRID_Y // rows_y
    groups = 2 * MODES_T
    per_group = 2 * HALF_Z
    kept_here = MODES_X // parts_y
    lanes = rows_x * rows_y
    pairs = samples * channels

    twiddle = plane_table()
    field = plume_field.reshape(pairs, lanes, STEPS_T, GRID_Z)
    spectrum = jnp.einsum("tzn,Bxtz->Bnx", twiddle, field, preferred_element_type=jnp.float32)
    spectrum = spectrum.reshape(samples, channels, groups, per_group, lanes)

    cosines, sines = line_parts(MODES_X, GRID_X)
    parts = jnp.stack([cosines, sines], axis=0).reshape(2, parts_y, kept_here, parts_x, rows_x)
    eye_y = jnp.eye(rows_y, dtype=jnp.float32)
    kron = parts[:, :, :, None, :, :, None] * eye_y[:, None, None, :]
    kron = jnp.transpose(kron, (4, 5, 6, 0, 1, 2, 3))
    kron = kron.reshape(parts_x, lanes, 2, parts_y, kept_here * rows_y)

    second = line_matrix(MODES_Y, GRID_Y).reshape(2, MODES_Y, 2, parts_y, rows_y)
    second = jnp.transpose(second, (3, 2, 4, 0, 1)).reshape(parts_y, 2 * rows_y, 1, 2 * MODES_Y)
    second = jnp.broadcast_to(second, (parts_y, 2 * rows_y, kept_here, 2 * MODES_Y))

    outs = []
    for sample in range(samples):
        moved = lax.all_to_all(spectrum[sample], "gx", 1, 1, tiled=False)
        outs.append(one_sample(moved, mode_weights, kron, second))
    return jnp.stack(outs, axis=0)


def solution(mesh):
    return jax.shard_map(
        local,
        mesh=mesh,
        in_specs=(P(None, None, "gx", "gy", None, None), P("gy", None, None, "gx", None, None)),
        out_specs=P(None, "gy", None, "gx", None, None),
        check_vma=False,
    )
```

```python
import math

import jax
import jax.numpy as jnp
from jax import lax
from jax.sharding import PartitionSpec as P

GRID_X = 128
GRID_Y = 128
GRID_Z = 128
STEPS_T = 16
MODES_X = 24
MODES_Y = 24
MODES_Z = 24
MODES_T = 8
HALF_Z = 12


def kept_modes(kept_count, axis_length):
    position = jnp.arange(kept_count, dtype=jnp.int32)
    return jnp.where(position < kept_count // 2, position, axis_length - kept_count + position)


def plane_table():
    moments = jnp.arange(STEPS_T, dtype=jnp.int32)
    depths = jnp.arange(GRID_Z, dtype=jnp.int32)
    time_freq = jnp.arange(MODES_T, dtype=jnp.int32)
    depth_freq = kept_modes(MODES_Z, GRID_Z).reshape(2, HALF_Z)
    phase_index = (
        time_freq[None, None, :, None, None]
        * moments[:, None, None, None, None]
        * (GRID_Z // STEPS_T)
        + depth_freq[None, None, None, :, :] * depths[None, :, None, None, None]
    ) % GRID_Z
    phases = 2.0 * math.pi / GRID_Z * phase_index.astype(jnp.float32)
    factor = 1.0 / math.sqrt(STEPS_T * GRID_Z)
    twiddle = jnp.stack([factor * jnp.cos(phases), -factor * jnp.sin(phases)], axis=4)
    return twiddle.reshape(STEPS_T, GRID_Z, 2 * MODES_T * MODES_Z).astype(jnp.bfloat16)


def line_parts(kept_count, axis_length):
    frequency = kept_modes(kept_count, axis_length)
    positions = jnp.arange(axis_length, dtype=jnp.int32)
    phase_index = frequency[:, None] * positions[None, :] % axis_length
    phases = 2.0 * math.pi / axis_length * phase_index.astype(jnp.float32)
    factor = 1.0 / math.sqrt(axis_length)
    return factor * jnp.cos(phases), factor * jnp.sin(phases)


def line_matrix(kept_count, axis_length):
    frequency = kept_modes(kept_count, axis_length)
    positions = jnp.arange(axis_length, dtype=jnp.int32)
    phase_index = frequency[:, None] * positions[None, :] % axis_length
    phases = 2.0 * math.pi / axis_length * phase_index.astype(jnp.float32)
    factor = 1.0 / math.sqrt(axis_length)
    cosines = factor * jnp.cos(phases)
    sines = factor * jnp.sin(phases)
    upper = jnp.stack([cosines, sines], axis=1)
    lower = jnp.stack([-sines, cosines], axis=1)
    return jnp.stack([upper, lower], axis=0)


def one_sample(moved, mode_weights, kron, second):
    high = lax.Precision.HIGH
    pairs, parts_x, _, lanes = moved.shape
    parts_y = second.shape[0]
    rows_y = second.shape[1] // 2
    kept_here = MODES_X // parts_y

    both = lax.dot_general(moved, kron, (((1, 3), (0, 1)), ((), ())), precision=high)
    both = both.reshape(pairs, 2, HALF_Z, 2, parts_y, kept_here * rows_y)
    out_re = both[:, 0, :, 0] + both[:, 1, :, 1]
    out_im = both[:, 1, :, 0] - both[:, 0, :, 1]
    after_x = jnp.stack([out_re, out_im], axis=0)
    after_x = after_x.reshape(2, pairs, HALF_Z, parts_y, kept_here, rows_y)
    after_x = jnp.transpose(after_x, (3, 4, 0, 5, 2, 1))
    after_x = after_x.reshape(parts_y, kept_here * 2 * rows_y, HALF_Z * pairs)
    gathered = lax.all_to_all(after_x, "gy", 0, 0, tiled=False)
    gathered = gathered.reshape(parts_y, kept_here, 2 * rows_y, HALF_Z * pairs)

    after_y = lax.dot_general(gathered, second, (((0, 2), (0, 1)), ((1,), (2,))), precision=high)
    after_y = after_y.reshape(kept_here, HALF_Z, pairs, 2, MODES_Y)
    after_y = jnp.transpose(after_y, (0, 2, 3, 1, 4))
    after_y = after_y.reshape(kept_here, pairs, 2, HALF_Z * MODES_Y)

    real_part = after_y[:, :, None, 0]
    imag_part = after_y[:, :, None, 1]
    weight_re = mode_weights[:, :, :, 0, 0].astype(jnp.float32)
    weight_im = mode_weights[:, :, :, 0, 1].astype(jnp.float32)
    mixed_re = jnp.sum(real_part * weight_re - imag_part * weight_im, axis=1)
    mixed_im = jnp.sum(real_part * weight_im + imag_part * weight_re, axis=1)
    return jnp.stack([mixed_re, mixed_im], axis=2)[:, :, None]


def local(plume_field, mode_weights):
    samples, channels, rows_x, rows_y = plume_field.shape[:4]
    parts_x = GRID_X // rows_x
    parts_y = GRID_Y // rows_y
    groups = 2 * MODES_T
    per_group = 2 * HALF_Z
    kept_here = MODES_X // parts_y
    lanes = rows_x * rows_y
    pairs = samples * channels

    twiddle = plane_table()
    field = plume_field.reshape(pairs, lanes, STEPS_T, GRID_Z)
    spectrum = jnp.einsum("tzn,Bxtz->Bnx", twiddle, field, preferred_element_type=jnp.float32)
    spectrum = spectrum.reshape(samples, channels, groups, per_group, lanes)

    cosines, sines = line_parts(MODES_X, GRID_X)
    parts = jnp.stack([cosines, sines], axis=0).reshape(2, parts_y, kept_here, parts_x, rows_x)
    eye_y = jnp.eye(rows_y, dtype=jnp.float32)
    kron = parts[:, :, :, None, :, :, None] * eye_y[:, None, None, :]
    kron = jnp.transpose(kron, (4, 5, 6, 0, 1, 2, 3))
    kron = kron.reshape(parts_x, lanes, 2, parts_y, kept_here * rows_y)

    second = line_matrix(MODES_Y, GRID_Y).reshape(2, MODES_Y, 2, parts_y, rows_y)
    second = jnp.transpose(second, (3, 2, 4, 0, 1)).reshape(parts_y, 2 * rows_y, 1, 2 * MODES_Y)
    second = jnp.broadcast_to(second, (parts_y, 2 * rows_y, kept_here, 2 * MODES_Y))

    chunks = [spectrum[sample] for sample in range(samples)]
    kron, chunks[1:] = lax.optimization_barrier((kron, chunks[1:]))
    outs = []
    for sample in range(samples):
        moved = lax.all_to_all(chunks[sample], "gx", 1, 1, tiled=False)
        outs.append(one_sample(moved, mode_weights, kron, second))
    return jnp.stack(outs, axis=0)


def solution(mesh):
    return jax.shard_map(
        local,
        mesh=mesh,
        in_specs=(P(None, None, "gx", "gy", None, None), P("gy", None, None, "gx", None, None)),
        out_specs=P(None, "gy", None, "gx", None, None),
        check_vma=False,
    )
```

```python
import math

import jax
import jax.numpy as jnp
from jax import lax
from jax.sharding import PartitionSpec as P

GRID_X = 128
GRID_Y = 128
GRID_Z = 128
STEPS_T = 16
MODES_X = 24
MODES_Y = 24
MODES_Z = 24
MODES_T = 8
HALF_Z = 12


def kept_modes(kept_count, axis_length):
    position = jnp.arange(kept_count, dtype=jnp.int32)
    return jnp.where(position < kept_count // 2, position, axis_length - kept_count + position)


def plane_table():
    moments = jnp.arange(STEPS_T, dtype=jnp.int32)
    depths = jnp.arange(GRID_Z, dtype=jnp.int32)
    time_freq = jnp.arange(MODES_T, dtype=jnp.int32)
    depth_freq = kept_modes(MODES_Z, GRID_Z).reshape(2, HALF_Z)
    phase_index = (
        time_freq[None, None, :, None, None]
        * moments[:, None, None, None, None]
        * (GRID_Z // STEPS_T)
        + depth_freq[None, None, None, :, :] * depths[None, :, None, None, None]
    ) % GRID_Z
    phases = 2.0 * math.pi / GRID_Z * phase_index.astype(jnp.float32)
    factor = 1.0 / math.sqrt(STEPS_T * GRID_Z)
    twiddle = jnp.stack([factor * jnp.cos(phases), -factor * jnp.sin(phases)], axis=4)
    return twiddle.reshape(STEPS_T, GRID_Z, 2 * MODES_T * MODES_Z).astype(jnp.bfloat16)


def line_parts(kept_count, axis_length):
    frequency = kept_modes(kept_count, axis_length)
    positions = jnp.arange(axis_length, dtype=jnp.int32)
    phase_index = frequency[:, None] * positions[None, :] % axis_length
    phases = 2.0 * math.pi / axis_length * phase_index.astype(jnp.float32)
    factor = 1.0 / math.sqrt(axis_length)
    return factor * jnp.cos(phases), factor * jnp.sin(phases)


def line_matrix(kept_count, axis_length):
    frequency = kept_modes(kept_count, axis_length)
    positions = jnp.arange(axis_length, dtype=jnp.int32)
    phase_index = frequency[:, None] * positions[None, :] % axis_length
    phases = 2.0 * math.pi / axis_length * phase_index.astype(jnp.float32)
    factor = 1.0 / math.sqrt(axis_length)
    cosines = factor * jnp.cos(phases)
    sines = factor * jnp.sin(phases)
    upper = jnp.stack([cosines, sines], axis=1)
    lower = jnp.stack([-sines, cosines], axis=1)
    return jnp.stack([upper, lower], axis=0)


def one_sample(moved, mode_weights, kron, second):
    high = lax.Precision.HIGH
    pairs, parts_x, _, lanes = moved.shape
    parts_y = second.shape[0]
    rows_y = second.shape[1] // 2
    kept_here = MODES_X // parts_y

    moved = moved.reshape(pairs, parts_x * 2, HALF_Z, lanes)
    after_x = lax.dot_general(kron, moved, (((1, 2), (1, 3)), ((), ())), precision=high)
    after_x = after_x.reshape(parts_y, kept_here * 2 * rows_y, pairs * HALF_Z)
    gathered = lax.all_to_all(after_x, "gy", 0, 0, tiled=False)
    gathered = gathered.reshape(parts_y, kept_here, 2 * rows_y, pairs * HALF_Z)

    after_y = lax.dot_general(gathered, second, (((0, 2), (0, 1)), ((1,), (2,))), precision=high)
    after_y = after_y.reshape(kept_here, pairs, HALF_Z, 2, MODES_Y)
    after_y = jnp.transpose(after_y, (0, 1, 3, 2, 4))
    after_y = after_y.reshape(kept_here, pairs, 2, HALF_Z * MODES_Y)

    real_part = after_y[:, :, None, 0]
    imag_part = after_y[:, :, None, 1]
    weight_re = mode_weights[:, :, :, 0, 0].astype(jnp.float32)
    weight_im = mode_weights[:, :, :, 0, 1].astype(jnp.float32)
    mixed_re = jnp.sum(real_part * weight_re - imag_part * weight_im, axis=1)
    mixed_im = jnp.sum(real_part * weight_im + imag_part * weight_re, axis=1)
    return jnp.stack([mixed_re, mixed_im], axis=2)[:, :, None]


def local(plume_field, mode_weights):
    samples, channels, rows_x, rows_y = plume_field.shape[:4]
    parts_x = GRID_X // rows_x
    parts_y = GRID_Y // rows_y
    groups = 2 * MODES_T
    per_group = 2 * HALF_Z
    kept_here = MODES_X // parts_y
    lanes = rows_x * rows_y
    pairs = samples * channels

    twiddle = plane_table()
    field = plume_field.reshape(pairs, lanes, STEPS_T, GRID_Z)
    spectrum = jnp.einsum("tzn,Bxtz->Bnx", twiddle, field, preferred_element_type=jnp.float32)
    spectrum = spectrum.reshape(samples, channels, groups, per_group, lanes)

    first = line_matrix(MODES_X, GRID_X).reshape(2, parts_y, kept_here, 2, parts_x, rows_x)
    first = jnp.transpose(first, (1, 2, 0, 4, 3, 5)).reshape(MODES_X * 2, parts_x * 2, rows_x)
    lane = jnp.arange(lanes, dtype=jnp.int32)
    spread = (lane[None, :] // rows_y == jnp.arange(rows_x, dtype=jnp.int32)[:, None]).astype(jnp.float32)
    keep = (lane[None, :] % rows_y == jnp.arange(rows_y, dtype=jnp.int32)[:, None]).astype(jnp.float32)
    spread_first = jnp.einsum("aip,pq->aiq", first, spread, precision=lax.Precision.HIGHEST)
    kron = spread_first[:, None] * keep[None, :, None, :]
    kron = kron.reshape(MODES_X * 2 * rows_y, parts_x * 2, lanes)

    second = line_matrix(MODES_Y, GRID_Y).reshape(2, MODES_Y, 2, parts_y, rows_y)
    second = jnp.transpose(second, (3, 2, 4, 0, 1)).reshape(parts_y, 2 * rows_y, 1, 2 * MODES_Y)
    second = jnp.broadcast_to(second, (parts_y, 2 * rows_y, kept_here, 2 * MODES_Y))

    chunks = [spectrum[sample] for sample in range(samples)]
    kron, chunks[1:] = lax.optimization_barrier((kron, chunks[1:]))
    outs = []
    for sample in range(samples):
        moved = lax.all_to_all(chunks[sample], "gx", 1, 1, tiled=False)
        outs.append(one_sample(moved, mode_weights, kron, second))
    return jnp.stack(outs, axis=0)


def solution(mesh):
    return jax.shard_map(
        local,
        mesh=mesh,
        in_specs=(P(None, None, "gx", "gy", None, None), P("gy", None, None, "gx", None, None)),
        out_specs=P(None, "gy", None, "gx", None, None),
        check_vma=False,
    )
```

```python
import math

import jax
import jax.numpy as jnp
from jax import lax
from jax.sharding import PartitionSpec as P

GRID_X = 128
GRID_Y = 128
GRID_Z = 128
STEPS_T = 16
MODES_X = 24
MODES_Y = 24
MODES_Z = 24
MODES_T = 8
HALF_Z = 12


def kept_modes(kept_count, axis_length):
    position = jnp.arange(kept_count, dtype=jnp.int32)
    return jnp.where(position < kept_count // 2, position, axis_length - kept_count + position)


def plane_table():
    moments = jnp.arange(STEPS_T, dtype=jnp.int32)
    depths = jnp.arange(GRID_Z, dtype=jnp.int32)
    time_freq = jnp.arange(MODES_T, dtype=jnp.int32)
    depth_freq = kept_modes(MODES_Z, GRID_Z).reshape(2, HALF_Z)
    phase_index = (
        time_freq[None, None, :, None, None]
        * moments[:, None, None, None, None]
        * (GRID_Z // STEPS_T)
        + depth_freq[None, None, None, :, :] * depths[None, :, None, None, None]
    ) % GRID_Z
    phases = 2.0 * math.pi / GRID_Z * phase_index.astype(jnp.float32)
    factor = 1.0 / math.sqrt(STEPS_T * GRID_Z)
    twiddle = jnp.stack([factor * jnp.cos(phases), -factor * jnp.sin(phases)], axis=4)
    return twiddle.reshape(STEPS_T, GRID_Z, 2 * MODES_T * MODES_Z).astype(jnp.bfloat16)


def line_parts(kept_count, axis_length):
    frequency = kept_modes(kept_count, axis_length)
    positions = jnp.arange(axis_length, dtype=jnp.int32)
    phase_index = frequency[:, None] * positions[None, :] % axis_length
    phases = 2.0 * math.pi / axis_length * phase_index.astype(jnp.float32)
    factor = 1.0 / math.sqrt(axis_length)
    return factor * jnp.cos(phases), factor * jnp.sin(phases)


def line_matrix(kept_count, axis_length):
    frequency = kept_modes(kept_count, axis_length)
    positions = jnp.arange(axis_length, dtype=jnp.int32)
    phase_index = frequency[:, None] * positions[None, :] % axis_length
    phases = 2.0 * math.pi / axis_length * phase_index.astype(jnp.float32)
    factor = 1.0 / math.sqrt(axis_length)
    cosines = factor * jnp.cos(phases)
    sines = factor * jnp.sin(phases)
    upper = jnp.stack([cosines, sines], axis=1)
    lower = jnp.stack([-sines, cosines], axis=1)
    return jnp.stack([upper, lower], axis=0)


def x_stage(moved, kron):
    high = lax.Precision.HIGH
    pairs, parts_x, _, lanes = moved.shape
    moved = moved.reshape(pairs, parts_x * 2, HALF_Z, lanes)
    after_x = lax.dot_general(kron, moved, (((1, 2), (1, 3)), ((), ())), precision=high)
    return after_x


def y_stage(after_x, mode_weights, second, samples, channels):
    high = lax.Precision.HIGH
    parts_y = second.shape[0]
    rows_y = second.shape[1] // 2
    kept_here = MODES_X // parts_y
    pairs = samples * channels
    after_x = after_x.reshape(parts_y, kept_here * 2 * rows_y, pairs * HALF_Z)
    gathered = lax.all_to_all(after_x, "gy", 0, 0, tiled=False)
    gathered = gathered.reshape(parts_y, kept_here, 2 * rows_y, pairs * HALF_Z)

    after_y = lax.dot_general(gathered, second, (((0, 2), (0, 1)), ((1,), (2,))), precision=high)
    after_y = after_y.reshape(kept_here, samples, channels, HALF_Z, 2, MODES_Y)
    after_y = jnp.transpose(after_y, (0, 1, 2, 4, 3, 5))
    after_y = after_y.reshape(kept_here, samples, channels, 2, HALF_Z * MODES_Y)

    real_part = after_y[:, :, :, None, 0]
    imag_part = after_y[:, :, :, None, 1]
    weight_re = mode_weights[:, None, :, :, 0, 0].astype(jnp.float32)
    weight_im = mode_weights[:, None, :, :, 0, 1].astype(jnp.float32)
    mixed_re = jnp.sum(real_part * weight_re - imag_part * weight_im, axis=2)
    mixed_im = jnp.sum(real_part * weight_im + imag_part * weight_re, axis=2)
    mixed = jnp.stack([mixed_re, mixed_im], axis=3)[:, :, :, None]
    return jnp.swapaxes(mixed, 0, 1)


def local(plume_field, mode_weights):
    samples, channels, rows_x, rows_y = plume_field.shape[:4]
    parts_x = GRID_X // rows_x
    parts_y = GRID_Y // rows_y
    groups = 2 * MODES_T
    per_group = 2 * HALF_Z
    kept_here = MODES_X // parts_y
    lanes = rows_x * rows_y
    pairs = samples * channels

    twiddle = plane_table()
    field = plume_field.reshape(pairs, lanes, STEPS_T, GRID_Z)
    spectrum = jnp.einsum("tzn,Bxtz->Bnx", twiddle, field, preferred_element_type=jnp.float32)
    spectrum = spectrum.reshape(samples, channels, groups, per_group, lanes)

    first = line_matrix(MODES_X, GRID_X).reshape(2, parts_y, kept_here, 2, parts_x, rows_x)
    first = jnp.transpose(first, (1, 2, 0, 4, 3, 5)).reshape(MODES_X * 2, parts_x * 2, rows_x)
    lane = jnp.arange(lanes, dtype=jnp.int32)
    spread = (lane[None, :] // rows_y == jnp.arange(rows_x, dtype=jnp.int32)[:, None]).astype(jnp.float32)
    keep = (lane[None, :] % rows_y == jnp.arange(rows_y, dtype=jnp.int32)[:, None]).astype(jnp.float32)
    spread_first = jnp.einsum("aip,pq->aiq", first, spread, precision=lax.Precision.HIGHEST)
    kron = spread_first[:, None] * keep[None, :, None, :]
    kron = kron.reshape(MODES_X * 2 * rows_y, parts_x * 2, lanes)

    second = line_matrix(MODES_Y, GRID_Y).reshape(2, MODES_Y, 2, parts_y, rows_y)
    second = jnp.transpose(second, (3, 2, 4, 0, 1)).reshape(parts_y, 2 * rows_y, 1, 2 * MODES_Y)
    second = jnp.broadcast_to(second, (parts_y, 2 * rows_y, kept_here, 2 * MODES_Y))

    splits = 2
    width = channels // splits
    spectrum = spectrum.reshape(samples * splits, width, groups, per_group, lanes)
    chunks = [spectrum[index] for index in range(samples * splits)]
    kron, chunks[1:] = lax.optimization_barrier((kron, chunks[1:]))
    payloads = []
    for chunk in chunks:
        moved = lax.all_to_all(chunk, "gx", 1, 1, tiled=False)
        payloads.append(x_stage(moved, kron))
    after_x = jnp.concatenate(payloads, axis=1)
    return y_stage(after_x, mode_weights, second, samples, channels)


def solution(mesh):
    return jax.shard_map(
        local,
        mesh=mesh,
        in_specs=(P(None, None, "gx", "gy", None, None), P("gy", None, None, "gx", None, None)),
        out_specs=P(None, "gy", None, "gx", None, None),
        check_vma=False,
    )
```

```python
import math

import jax
import jax.numpy as jnp
from jax import lax
from jax.sharding import PartitionSpec as P

GRID_X = 128
GRID_Y = 128
GRID_Z = 128
STEPS_T = 16
MODES_X = 24
MODES_Y = 24
MODES_Z = 24
MODES_T = 8
HALF_Z = 12


def kept_modes(kept_count, axis_length):
    position = jnp.arange(kept_count, dtype=jnp.int32)
    return jnp.where(position < kept_count // 2, position, axis_length - kept_count + position)


def plane_table():
    moments = jnp.arange(STEPS_T, dtype=jnp.int32)
    depths = jnp.arange(GRID_Z, dtype=jnp.int32)
    time_freq = jnp.arange(MODES_T, dtype=jnp.int32)
    depth_freq = kept_modes(MODES_Z, GRID_Z).reshape(2, HALF_Z)
    phase_index = (
        time_freq[None, None, :, None, None]
        * moments[:, None, None, None, None]
        * (GRID_Z // STEPS_T)
        + depth_freq[None, None, None, :, :] * depths[None, :, None, None, None]
    ) % GRID_Z
    phases = 2.0 * math.pi / GRID_Z * phase_index.astype(jnp.float32)
    factor = 1.0 / math.sqrt(STEPS_T * GRID_Z)
    twiddle = jnp.stack([factor * jnp.cos(phases), -factor * jnp.sin(phases)], axis=4)
    return twiddle.reshape(STEPS_T, GRID_Z, 2 * MODES_T * MODES_Z).astype(jnp.bfloat16)


def line_parts(kept_count, axis_length):
    frequency = kept_modes(kept_count, axis_length)
    positions = jnp.arange(axis_length, dtype=jnp.int32)
    phase_index = frequency[:, None] * positions[None, :] % axis_length
    phases = 2.0 * math.pi / axis_length * phase_index.astype(jnp.float32)
    factor = 1.0 / math.sqrt(axis_length)
    return factor * jnp.cos(phases), factor * jnp.sin(phases)


def line_matrix(kept_count, axis_length):
    frequency = kept_modes(kept_count, axis_length)
    positions = jnp.arange(axis_length, dtype=jnp.int32)
    phase_index = frequency[:, None] * positions[None, :] % axis_length
    phases = 2.0 * math.pi / axis_length * phase_index.astype(jnp.float32)
    factor = 1.0 / math.sqrt(axis_length)
    cosines = factor * jnp.cos(phases)
    sines = factor * jnp.sin(phases)
    upper = jnp.stack([cosines, sines], axis=1)
    lower = jnp.stack([-sines, cosines], axis=1)
    return jnp.stack([upper, lower], axis=0)


def one_sample(moved, mode_weights, kron, second):
    high = lax.Precision.HIGH
    pairs, parts_x, _, lanes = moved.shape
    parts_y = second.shape[0]
    rows_y = second.shape[1] // 2
    kept_here = MODES_X // parts_y

    moved = moved.reshape(pairs, parts_x * 2, HALF_Z, lanes)
    upper = moved.astype(jnp.bfloat16)
    lower = (moved - upper.astype(jnp.float32)).astype(jnp.bfloat16)
    numbers = (((1, 2), (1, 3)), ((), ()))
    after_x = lax.dot_general(kron, upper, numbers, preferred_element_type=jnp.float32) + lax.dot_general(
        kron, lower, numbers, preferred_element_type=jnp.float32
    )
    after_x = after_x.reshape(parts_y, kept_here * 2 * rows_y, pairs * HALF_Z)
    gathered = lax.all_to_all(after_x, "gy", 0, 0, tiled=False)
    gathered = gathered.reshape(parts_y, kept_here, 2 * rows_y, pairs * HALF_Z)

    after_y = lax.dot_general(gathered, second, (((0, 2), (0, 1)), ((1,), (2,))), precision=high)
    after_y = after_y.reshape(kept_here, pairs, HALF_Z, 2, MODES_Y)
    after_y = jnp.transpose(after_y, (0, 1, 3, 2, 4))
    after_y = after_y.reshape(kept_here, pairs, 2, HALF_Z * MODES_Y)

    real_part = after_y[:, :, None, 0]
    imag_part = after_y[:, :, None, 1]
    weight_re = mode_weights[:, :, :, 0, 0].astype(jnp.float32)
    weight_im = mode_weights[:, :, :, 0, 1].astype(jnp.float32)
    mixed_re = jnp.sum(real_part * weight_re - imag_part * weight_im, axis=1)
    mixed_im = jnp.sum(real_part * weight_im + imag_part * weight_re, axis=1)
    return jnp.stack([mixed_re, mixed_im], axis=2)[:, :, None]


def local(plume_field, mode_weights):
    samples, channels, rows_x, rows_y = plume_field.shape[:4]
    parts_x = GRID_X // rows_x
    parts_y = GRID_Y // rows_y
    groups = 2 * MODES_T
    per_group = 2 * HALF_Z
    kept_here = MODES_X // parts_y
    lanes = rows_x * rows_y
    pairs = samples * channels

    twiddle = plane_table()
    field = plume_field.reshape(pairs, lanes, STEPS_T, GRID_Z)
    spectrum = jnp.einsum("tzn,Bxtz->Bnx", twiddle, field, preferred_element_type=jnp.float32)
    spectrum = spectrum.reshape(samples, channels, groups, per_group, lanes)

    first = line_matrix(MODES_X, GRID_X).reshape(2, parts_y, kept_here, 2, parts_x, rows_x)
    first = jnp.transpose(first, (1, 2, 0, 4, 3, 5)).reshape(MODES_X * 2, parts_x * 2, rows_x)
    lane = jnp.arange(lanes, dtype=jnp.int32)
    spread = (lane[None, :] // rows_y == jnp.arange(rows_x, dtype=jnp.int32)[:, None]).astype(jnp.float32)
    keep = (lane[None, :] % rows_y == jnp.arange(rows_y, dtype=jnp.int32)[:, None]).astype(jnp.float32)
    spread_first = jnp.einsum("aip,pq->aiq", first, spread, precision=lax.Precision.HIGHEST)
    kron = spread_first[:, None] * keep[None, :, None, :]
    kron = kron.reshape(MODES_X * 2 * rows_y, parts_x * 2, lanes).astype(jnp.bfloat16)

    second = line_matrix(MODES_Y, GRID_Y).reshape(2, MODES_Y, 2, parts_y, rows_y)
    second = jnp.transpose(second, (3, 2, 4, 0, 1)).reshape(parts_y, 2 * rows_y, 1, 2 * MODES_Y)
    second = jnp.broadcast_to(second, (parts_y, 2 * rows_y, kept_here, 2 * MODES_Y))

    chunks = [spectrum[sample] for sample in range(samples)]
    kron, chunks[1:] = lax.optimization_barrier((kron, chunks[1:]))
    outs = []
    for sample in range(samples):
        moved = lax.all_to_all(chunks[sample], "gx", 1, 1, tiled=False)
        outs.append(one_sample(moved, mode_weights, kron, second))
    return jnp.stack(outs, axis=0)


def solution(mesh):
    return jax.shard_map(
        local,
        mesh=mesh,
        in_specs=(P(None, None, "gx", "gy", None, None), P("gy", None, None, "gx", None, None)),
        out_specs=P(None, "gy", None, "gx", None, None),
        check_vma=False,
    )
```

```python
import math

import jax
import jax.numpy as jnp
from jax import lax
from jax.sharding import PartitionSpec as P

GRID_X = 128
GRID_Y = 128
GRID_Z = 128
STEPS_T = 16
MODES_X = 24
MODES_Y = 24
MODES_Z = 24
MODES_T = 8
HALF_Z = 12


def kept_modes(kept_count, axis_length):
    position = jnp.arange(kept_count, dtype=jnp.int32)
    return jnp.where(position < kept_count // 2, position, axis_length - kept_count + position)


def plane_table():
    moments = jnp.arange(STEPS_T, dtype=jnp.int32)
    depths = jnp.arange(GRID_Z, dtype=jnp.int32)
    time_freq = jnp.arange(MODES_T, dtype=jnp.int32)
    depth_freq = kept_modes(MODES_Z, GRID_Z).reshape(2, HALF_Z)
    phase_index = (
        time_freq[None, None, :, None, None]
        * moments[:, None, None, None, None]
        * (GRID_Z // STEPS_T)
        + depth_freq[None, None, None, :, :] * depths[None, :, None, None, None]
    ) % GRID_Z
    phases = 2.0 * math.pi / GRID_Z * phase_index.astype(jnp.float32)
    factor = 1.0 / math.sqrt(STEPS_T * GRID_Z)
    twiddle = jnp.stack([factor * jnp.cos(phases), -factor * jnp.sin(phases)], axis=4)
    return twiddle.reshape(STEPS_T, GRID_Z, 2 * MODES_T * MODES_Z).astype(jnp.bfloat16)


def line_parts(kept_count, axis_length):
    frequency = kept_modes(kept_count, axis_length)
    positions = jnp.arange(axis_length, dtype=jnp.int32)
    phase_index = frequency[:, None] * positions[None, :] % axis_length
    phases = 2.0 * math.pi / axis_length * phase_index.astype(jnp.float32)
    factor = 1.0 / math.sqrt(axis_length)
    return factor * jnp.cos(phases), factor * jnp.sin(phases)


def line_matrix(kept_count, axis_length):
    frequency = kept_modes(kept_count, axis_length)
    positions = jnp.arange(axis_length, dtype=jnp.int32)
    phase_index = frequency[:, None] * positions[None, :] % axis_length
    phases = 2.0 * math.pi / axis_length * phase_index.astype(jnp.float32)
    factor = 1.0 / math.sqrt(axis_length)
    cosines = factor * jnp.cos(phases)
    sines = factor * jnp.sin(phases)
    upper = jnp.stack([cosines, sines], axis=1)
    lower = jnp.stack([-sines, cosines], axis=1)
    return jnp.stack([upper, lower], axis=0)


def one_sample(moved, mode_weights, kron, second):
    high = lax.Precision.HIGH
    pairs, parts_x, _, lanes = moved.shape
    parts_y = second.shape[0]
    rows_y = second.shape[1] // 2
    kept_here = MODES_X // parts_y

    moved = moved.reshape(pairs, parts_x * 2, HALF_Z, lanes)
    upper = moved.astype(jnp.bfloat16)
    lower = (moved - upper.astype(jnp.float32)).astype(jnp.bfloat16)
    numbers = (((1, 2), (1, 3)), ((), ()))
    kron_upper, kron_lower = kron
    after_x = (
        lax.dot_general(kron_upper, upper, numbers, preferred_element_type=jnp.float32)
        + lax.dot_general(kron_upper, lower, numbers, preferred_element_type=jnp.float32)
        + lax.dot_general(kron_lower, upper, numbers, preferred_element_type=jnp.float32)
    )
    after_x = after_x.reshape(parts_y, kept_here * 2 * rows_y, pairs * HALF_Z)
    gathered = lax.all_to_all(after_x, "gy", 0, 0, tiled=False)
    gathered = gathered.reshape(parts_y, kept_here, 2 * rows_y, pairs * HALF_Z)

    after_y = lax.dot_general(gathered, second, (((0, 2), (0, 1)), ((1,), (2,))), precision=high)
    after_y = after_y.reshape(kept_here, pairs, HALF_Z, 2, MODES_Y)
    after_y = jnp.transpose(after_y, (0, 1, 3, 2, 4))
    after_y = after_y.reshape(kept_here, pairs, 2, HALF_Z * MODES_Y)

    real_part = after_y[:, :, None, 0]
    imag_part = after_y[:, :, None, 1]
    weight_re = mode_weights[:, :, :, 0, 0].astype(jnp.float32)
    weight_im = mode_weights[:, :, :, 0, 1].astype(jnp.float32)
    mixed_re = jnp.sum(real_part * weight_re - imag_part * weight_im, axis=1)
    mixed_im = jnp.sum(real_part * weight_im + imag_part * weight_re, axis=1)
    return jnp.stack([mixed_re, mixed_im], axis=2)[:, :, None]


def local(plume_field, mode_weights):
    samples, channels, rows_x, rows_y = plume_field.shape[:4]
    parts_x = GRID_X // rows_x
    parts_y = GRID_Y // rows_y
    groups = 2 * MODES_T
    per_group = 2 * HALF_Z
    kept_here = MODES_X // parts_y
    lanes = rows_x * rows_y
    pairs = samples * channels

    twiddle = plane_table()
    field = plume_field.reshape(pairs, lanes, STEPS_T, GRID_Z)
    spectrum = jnp.einsum("tzn,Bxtz->Bnx", twiddle, field, preferred_element_type=jnp.float32)
    spectrum = spectrum.reshape(samples, channels, groups, per_group, lanes)

    first = line_matrix(MODES_X, GRID_X).reshape(2, parts_y, kept_here, 2, parts_x, rows_x)
    first = jnp.transpose(first, (1, 2, 0, 4, 3, 5)).reshape(MODES_X * 2, parts_x * 2, rows_x)
    lane = jnp.arange(lanes, dtype=jnp.int32)
    spread = (lane[None, :] // rows_y == jnp.arange(rows_x, dtype=jnp.int32)[:, None]).astype(jnp.float32)
    keep = (lane[None, :] % rows_y == jnp.arange(rows_y, dtype=jnp.int32)[:, None]).astype(jnp.float32)
    spread_first = jnp.einsum("aip,pq->aiq", first, spread, precision=lax.Precision.HIGHEST)
    kron = spread_first[:, None] * keep[None, :, None, :]
    kron = kron.reshape(MODES_X * 2 * rows_y, parts_x * 2, lanes)
    kron_upper = kron.astype(jnp.bfloat16)
    kron = (kron_upper, (kron - kron_upper.astype(jnp.float32)).astype(jnp.bfloat16))

    second = line_matrix(MODES_Y, GRID_Y).reshape(2, MODES_Y, 2, parts_y, rows_y)
    second = jnp.transpose(second, (3, 2, 4, 0, 1)).reshape(parts_y, 2 * rows_y, 1, 2 * MODES_Y)
    second = jnp.broadcast_to(second, (parts_y, 2 * rows_y, kept_here, 2 * MODES_Y))

    chunks = [spectrum[sample] for sample in range(samples)]
    kron, chunks[1:] = lax.optimization_barrier((kron, chunks[1:]))
    outs = []
    for sample in range(samples):
        moved = lax.all_to_all(chunks[sample], "gx", 1, 1, tiled=False)
        outs.append(one_sample(moved, mode_weights, kron, second))
    return jnp.stack(outs, axis=0)


def solution(mesh):
    return jax.shard_map(
        local,
        mesh=mesh,
        in_specs=(P(None, None, "gx", "gy", None, None), P("gy", None, None, "gx", None, None)),
        out_specs=P(None, "gy", None, "gx", None, None),
        check_vma=False,
    )
```

```python
import math

import jax
import jax.numpy as jnp
from jax import lax
from jax.sharding import PartitionSpec as P

GRID_X = 128
GRID_Y = 128
GRID_Z = 128
STEPS_T = 16
MODES_X = 24
MODES_Y = 24
MODES_Z = 24
MODES_T = 8
HALF_Z = 12


def kept_modes(kept_count, axis_length):
    position = jnp.arange(kept_count, dtype=jnp.int32)
    return jnp.where(position < kept_count // 2, position, axis_length - kept_count + position)


def plane_table():
    moments = jnp.arange(STEPS_T, dtype=jnp.int32)
    depths = jnp.arange(GRID_Z, dtype=jnp.int32)
    time_freq = jnp.arange(MODES_T, dtype=jnp.int32)
    depth_freq = kept_modes(MODES_Z, GRID_Z).reshape(2, HALF_Z)
    phase_index = (
        time_freq[None, None, :, None, None]
        * moments[:, None, None, None, None]
        * (GRID_Z // STEPS_T)
        + depth_freq[None, None, None, :, :] * depths[None, :, None, None, None]
    ) % GRID_Z
    phases = 2.0 * math.pi / GRID_Z * phase_index.astype(jnp.float32)
    factor = 1.0 / math.sqrt(STEPS_T * GRID_Z)
    twiddle = jnp.stack([factor * jnp.cos(phases), -factor * jnp.sin(phases)], axis=4)
    return twiddle.reshape(STEPS_T, GRID_Z, 2 * MODES_T * MODES_Z).astype(jnp.bfloat16)


def line_parts(kept_count, axis_length):
    frequency = kept_modes(kept_count, axis_length)
    positions = jnp.arange(axis_length, dtype=jnp.int32)
    phase_index = frequency[:, None] * positions[None, :] % axis_length
    phases = 2.0 * math.pi / axis_length * phase_index.astype(jnp.float32)
    factor = 1.0 / math.sqrt(axis_length)
    return factor * jnp.cos(phases), factor * jnp.sin(phases)


def line_matrix(kept_count, axis_length):
    frequency = kept_modes(kept_count, axis_length)
    positions = jnp.arange(axis_length, dtype=jnp.int32)
    phase_index = frequency[:, None] * positions[None, :] % axis_length
    phases = 2.0 * math.pi / axis_length * phase_index.astype(jnp.float32)
    factor = 1.0 / math.sqrt(axis_length)
    cosines = factor * jnp.cos(phases)
    sines = factor * jnp.sin(phases)
    upper = jnp.stack([cosines, sines], axis=1)
    lower = jnp.stack([-sines, cosines], axis=1)
    return jnp.stack([upper, lower], axis=0)


def plane_table_fast():
    moments = jnp.arange(STEPS_T, dtype=jnp.int32)
    depths = jnp.arange(GRID_Z, dtype=jnp.int32)
    time_freq = jnp.arange(MODES_T, dtype=jnp.int32)
    depth_freq = kept_modes(MODES_Z, GRID_Z)
    step = 2.0 * math.pi / GRID_Z
    time_phase = step * ((moments[:, None] * time_freq[None, :] * (GRID_Z // STEPS_T)) % GRID_Z).astype(jnp.float32)
    depth_phase = step * ((depths[:, None] * depth_freq[None, :]) % GRID_Z).astype(jnp.float32)
    factor = 1.0 / math.sqrt(STEPS_T * GRID_Z)
    ct = (factor * jnp.cos(time_phase))[:, None, :, None]
    st = (factor * jnp.sin(time_phase))[:, None, :, None]
    cz = jnp.cos(depth_phase)[None, :, None, :]
    sz = jnp.sin(depth_phase)[None, :, None, :]
    cos_part = ct * cz - st * sz
    sin_part = st * cz + ct * sz
    twiddle = jnp.stack([cos_part.reshape(STEPS_T, GRID_Z, MODES_T, 2, HALF_Z),
                         -sin_part.reshape(STEPS_T, GRID_Z, MODES_T, 2, HALF_Z)], axis=4)
    return twiddle.reshape(STEPS_T, GRID_Z, 2 * MODES_T * MODES_Z).astype(jnp.bfloat16)


def one_sample(moved, mode_weights, kron, second):
    high = lax.Precision.HIGH
    pairs, parts_x, _, lanes = moved.shape
    parts_y = second.shape[0]
    rows_y = second.shape[1] // 2
    kept_here = MODES_X // parts_y

    moved = moved.reshape(pairs, parts_x * 2, HALF_Z, lanes)
    upper = moved.astype(jnp.bfloat16)
    lower = (moved - upper.astype(jnp.float32)).astype(jnp.bfloat16)
    numbers = (((1, 2), (1, 3)), ((), ()))
    kron_upper, kron_lower = kron
    after_x = (
        lax.dot_general(kron_upper, upper, numbers, preferred_element_type=jnp.float32)
        + lax.dot_general(kron_upper, lower, numbers, preferred_element_type=jnp.float32)
        + lax.dot_general(kron_lower, upper, numbers, preferred_element_type=jnp.float32)
    )
    after_x = after_x.reshape(parts_y, kept_here * 2 * rows_y, pairs * HALF_Z)
    gathered = lax.all_to_all(after_x, "gy", 0, 0, tiled=False)
    gathered = gathered.reshape(parts_y, kept_here, 2 * rows_y, pairs * HALF_Z)

    after_y = lax.dot_general(gathered, second, (((0, 2), (0, 1)), ((1,), (2,))), precision=high)
    after_y = after_y.reshape(kept_here, pairs, HALF_Z, 2, MODES_Y)
    after_y = jnp.transpose(after_y, (0, 1, 3, 2, 4))
    after_y = after_y.reshape(kept_here, pairs, 2, HALF_Z * MODES_Y)

    real_part = after_y[:, :, None, 0]
    imag_part = after_y[:, :, None, 1]
    weight_re = mode_weights[:, :, :, 0, 0].astype(jnp.float32)
    weight_im = mode_weights[:, :, :, 0, 1].astype(jnp.float32)
    mixed_re = jnp.sum(real_part * weight_re - imag_part * weight_im, axis=1)
    mixed_im = jnp.sum(real_part * weight_im + imag_part * weight_re, axis=1)
    return jnp.stack([mixed_re, mixed_im], axis=2)[:, :, None]


def local(plume_field, mode_weights):
    samples, channels, rows_x, rows_y = plume_field.shape[:4]
    parts_x = GRID_X // rows_x
    parts_y = GRID_Y // rows_y
    groups = 2 * MODES_T
    per_group = 2 * HALF_Z
    kept_here = MODES_X // parts_y
    lanes = rows_x * rows_y
    pairs = samples * channels

    twiddle = plane_table_fast()
    field = plume_field.reshape(pairs, lanes, STEPS_T, GRID_Z)
    spectrum = jnp.einsum("tzn,Bxtz->Bnx", twiddle, field, preferred_element_type=jnp.float32)
    spectrum = spectrum.reshape(samples, channels, groups, per_group, lanes)

    first = line_matrix(MODES_X, GRID_X).reshape(2, parts_y, kept_here, 2, parts_x, rows_x)
    first = jnp.transpose(first, (1, 2, 0, 4, 3, 5)).reshape(MODES_X * 2, parts_x * 2, rows_x)
    lane = jnp.arange(lanes, dtype=jnp.int32)
    spread = (lane[None, :] // rows_y == jnp.arange(rows_x, dtype=jnp.int32)[:, None]).astype(jnp.float32)
    keep = (lane[None, :] % rows_y == jnp.arange(rows_y, dtype=jnp.int32)[:, None]).astype(jnp.float32)
    spread_first = jnp.einsum("aip,pq->aiq", first, spread, precision=lax.Precision.HIGHEST)
    kron = spread_first[:, None] * keep[None, :, None, :]
    kron = kron.reshape(MODES_X * 2 * rows_y, parts_x * 2, lanes)
    kron_upper = kron.astype(jnp.bfloat16)
    kron = (kron_upper, (kron - kron_upper.astype(jnp.float32)).astype(jnp.bfloat16))

    second = line_matrix(MODES_Y, GRID_Y).reshape(2, MODES_Y, 2, parts_y, rows_y)
    second = jnp.transpose(second, (3, 2, 4, 0, 1)).reshape(parts_y, 2 * rows_y, 1, 2 * MODES_Y)
    second = jnp.broadcast_to(second, (parts_y, 2 * rows_y, kept_here, 2 * MODES_Y))

    chunks = [spectrum[sample] for sample in range(samples)]
    kron, chunks[1:] = lax.optimization_barrier((kron, chunks[1:]))
    outs = []
    for sample in range(samples):
        moved = lax.all_to_all(chunks[sample], "gx", 1, 1, tiled=False)
        outs.append(one_sample(moved, mode_weights, kron, second))
    return jnp.stack(outs, axis=0)


def solution(mesh):
    return jax.shard_map(
        local,
        mesh=mesh,
        in_specs=(P(None, None, "gx", "gy", None, None), P("gy", None, None, "gx", None, None)),
        out_specs=P(None, "gy", None, "gx", None, None),
        check_vma=False,
    )
```

```python
import math

import jax
import jax.numpy as jnp
from jax import lax
from jax.sharding import PartitionSpec as P

GRID_X = 128
GRID_Y = 128
GRID_Z = 128
STEPS_T = 16
MODES_X = 24
MODES_Y = 24
MODES_Z = 24
MODES_T = 8
HALF_Z = 12


def kept_modes(kept_count, axis_length):
    position = jnp.arange(kept_count, dtype=jnp.int32)
    return jnp.where(position < kept_count // 2, position, axis_length - kept_count + position)


def plane_table():
    moments = jnp.arange(STEPS_T, dtype=jnp.int32)
    depths = jnp.arange(GRID_Z, dtype=jnp.int32)
    time_freq = jnp.arange(MODES_T, dtype=jnp.int32)
    depth_freq = kept_modes(MODES_Z, GRID_Z).reshape(2, HALF_Z)
    phase_index = (
        time_freq[None, None, :, None, None]
        * moments[:, None, None, None, None]
        * (GRID_Z // STEPS_T)
        + depth_freq[None, None, None, :, :] * depths[None, :, None, None, None]
    ) % GRID_Z
    phases = 2.0 * math.pi / GRID_Z * phase_index.astype(jnp.float32)
    factor = 1.0 / math.sqrt(STEPS_T * GRID_Z)
    twiddle = jnp.stack([factor * jnp.cos(phases), -factor * jnp.sin(phases)], axis=4)
    return twiddle.reshape(STEPS_T, GRID_Z, 2 * MODES_T * MODES_Z).astype(jnp.bfloat16)


def line_parts(kept_count, axis_length):
    frequency = kept_modes(kept_count, axis_length)
    positions = jnp.arange(axis_length, dtype=jnp.int32)
    phase_index = frequency[:, None] * positions[None, :] % axis_length
    phases = 2.0 * math.pi / axis_length * phase_index.astype(jnp.float32)
    factor = 1.0 / math.sqrt(axis_length)
    return factor * jnp.cos(phases), factor * jnp.sin(phases)


def line_matrix(kept_count, axis_length):
    frequency = kept_modes(kept_count, axis_length)
    positions = jnp.arange(axis_length, dtype=jnp.int32)
    phase_index = frequency[:, None] * positions[None, :] % axis_length
    phases = 2.0 * math.pi / axis_length * phase_index.astype(jnp.float32)
    factor = 1.0 / math.sqrt(axis_length)
    cosines = factor * jnp.cos(phases)
    sines = factor * jnp.sin(phases)
    upper = jnp.stack([cosines, sines], axis=1)
    lower = jnp.stack([-sines, cosines], axis=1)
    return jnp.stack([upper, lower], axis=0)


def plane_table_fast():
    moments = jnp.arange(STEPS_T, dtype=jnp.int32)
    depths = jnp.arange(GRID_Z, dtype=jnp.int32)
    time_freq = jnp.arange(MODES_T, dtype=jnp.int32)
    depth_freq = kept_modes(MODES_Z, GRID_Z)
    step = 2.0 * math.pi / GRID_Z
    time_phase = step * ((moments[:, None] * time_freq[None, :] * (GRID_Z // STEPS_T)) % GRID_Z).astype(jnp.float32)
    depth_phase = step * ((depths[:, None] * depth_freq[None, :]) % GRID_Z).astype(jnp.float32)
    factor = 1.0 / math.sqrt(STEPS_T * GRID_Z)
    ct = (factor * jnp.cos(time_phase))[:, None, :, None]
    st = (factor * jnp.sin(time_phase))[:, None, :, None]
    cz = jnp.cos(depth_phase)[None, :, None, :]
    sz = jnp.sin(depth_phase)[None, :, None, :]
    cos_part = ct * cz - st * sz
    sin_part = st * cz + ct * sz
    twiddle = jnp.stack([cos_part.reshape(STEPS_T, GRID_Z, MODES_T, 2, HALF_Z),
                         -sin_part.reshape(STEPS_T, GRID_Z, MODES_T, 2, HALF_Z)], axis=4)
    return twiddle.reshape(STEPS_T, GRID_Z, 2 * MODES_T * MODES_Z).astype(jnp.bfloat16)


def one_sample(moved, mode_weights, kron, second):
    high = lax.Precision.HIGH
    pairs, parts_x, _, lanes = moved.shape
    parts_y = second.shape[0]
    rows_y = second.shape[1] // 2
    kept_here = MODES_X // parts_y

    moved = moved.reshape(pairs, parts_x * 2, HALF_Z, lanes)
    upper = moved.astype(jnp.bfloat16)
    lower = (moved - upper.astype(jnp.float32)).astype(jnp.bfloat16)
    numbers = (((1, 2), (1, 3)), ((), ()))
    kron_upper, kron_lower = kron
    after_x = (
        lax.dot_general(kron_upper, upper, numbers, preferred_element_type=jnp.float32)
        + lax.dot_general(kron_upper, lower, numbers, preferred_element_type=jnp.float32)
        + lax.dot_general(kron_lower, upper, numbers, preferred_element_type=jnp.float32)
    )
    after_x = after_x.reshape(parts_y, kept_here * 2 * rows_y, pairs * HALF_Z)
    gathered = lax.all_to_all(after_x, "gy", 0, 0, tiled=False)
    gathered = gathered.reshape(parts_y, kept_here, 2 * rows_y, pairs * HALF_Z)

    after_y = lax.dot_general(gathered, second, (((0, 2), (0, 1)), ((1,), (2,))), precision=high)
    after_y = after_y.reshape(kept_here, pairs, HALF_Z, 2, MODES_Y)
    after_y = jnp.transpose(after_y, (0, 1, 3, 2, 4))
    after_y = after_y.reshape(kept_here, pairs, 2, HALF_Z * MODES_Y)

    real_part = after_y[:, :, None, 0]
    imag_part = after_y[:, :, None, 1]
    weight_re = mode_weights[:, :, :, 0, 0].astype(jnp.float32)
    weight_im = mode_weights[:, :, :, 0, 1].astype(jnp.float32)
    mixed_re = jnp.sum(real_part * weight_re - imag_part * weight_im, axis=1)
    mixed_im = jnp.sum(real_part * weight_im + imag_part * weight_re, axis=1)
    return jnp.stack([mixed_re, mixed_im], axis=2)[:, :, None]


def local(plume_field, mode_weights):
    samples, channels, rows_x, rows_y = plume_field.shape[:4]
    parts_x = GRID_X // rows_x
    parts_y = GRID_Y // rows_y
    groups = 2 * MODES_T
    per_group = 2 * HALF_Z
    kept_here = MODES_X // parts_y
    lanes = rows_x * rows_y
    pairs = samples * channels

    twiddle = plane_table_fast()
    field = plume_field.reshape(pairs, lanes, STEPS_T, GRID_Z)
    spectrum = jnp.einsum("tzn,Bxtz->Bnx", twiddle, field, preferred_element_type=jnp.float32)
    spectrum = spectrum.reshape(samples, channels, groups, per_group, lanes)

    second = line_matrix(MODES_Y, GRID_Y).reshape(2, MODES_Y, 2, parts_y, rows_y)
    second = jnp.transpose(second, (3, 2, 4, 0, 1)).reshape(parts_y, 2 * rows_y, 1, 2 * MODES_Y)
    second = jnp.broadcast_to(second, (parts_y, 2 * rows_y, kept_here, 2 * MODES_Y))

    chunks = [spectrum[sample] for sample in range(samples)]
    first = line_matrix(MODES_X, GRID_X).reshape(2, parts_y, kept_here, 2, parts_x, rows_x)
    outs = []
    for sample in range(samples):
        moved = lax.all_to_all(chunks[sample], "gx", 1, 1, tiled=False)
        if sample == 0:
            first, moved = lax.optimization_barrier((first, moved))
            first = jnp.transpose(first, (1, 2, 0, 4, 3, 5)).reshape(MODES_X * 2, parts_x * 2, rows_x)
            lane = jnp.arange(lanes, dtype=jnp.int32)
            spread = (lane[None, :] // rows_y == jnp.arange(rows_x, dtype=jnp.int32)[:, None]).astype(jnp.float32)
            keep = (lane[None, :] % rows_y == jnp.arange(rows_y, dtype=jnp.int32)[:, None]).astype(jnp.float32)
            spread_first = jnp.einsum("aip,pq->aiq", first, spread, precision=lax.Precision.HIGHEST)
            kron = spread_first[:, None] * keep[None, :, None, :]
            kron = kron.reshape(MODES_X * 2 * rows_y, parts_x * 2, lanes)
            kron_upper = kron.astype(jnp.bfloat16)
            kron = (kron_upper, (kron - kron_upper.astype(jnp.float32)).astype(jnp.bfloat16))
        outs.append(one_sample(moved, mode_weights, kron, second))
    return jnp.stack(outs, axis=0)


def solution(mesh):
    return jax.shard_map(
        local,
        mesh=mesh,
        in_specs=(P(None, None, "gx", "gy", None, None), P("gy", None, None, "gx", None, None)),
        out_specs=P(None, "gy", None, "gx", None, None),
        check_vma=False,
    )
```

```python
import math

import jax
import jax.numpy as jnp
from jax import lax
from jax.sharding import PartitionSpec as P

GRID_X = 128
GRID_Y = 128
GRID_Z = 128
STEPS_T = 16
MODES_X = 24
MODES_Y = 24
MODES_Z = 24
MODES_T = 8
HALF_Z = 12


def kept_modes(kept_count, axis_length):
    position = jnp.arange(kept_count, dtype=jnp.int32)
    return jnp.where(position < kept_count // 2, position, axis_length - kept_count + position)


def plane_table():
    moments = jnp.arange(STEPS_T, dtype=jnp.int32)
    depths = jnp.arange(GRID_Z, dtype=jnp.int32)
    time_freq = jnp.arange(MODES_T, dtype=jnp.int32)
    depth_freq = kept_modes(MODES_Z, GRID_Z).reshape(2, HALF_Z)
    phase_index = (
        time_freq[None, None, :, None, None]
        * moments[:, None, None, None, None]
        * (GRID_Z // STEPS_T)
        + depth_freq[None, None, None, :, :] * depths[None, :, None, None, None]
    ) % GRID_Z
    phases = 2.0 * math.pi / GRID_Z * phase_index.astype(jnp.float32)
    factor = 1.0 / math.sqrt(STEPS_T * GRID_Z)
    twiddle = jnp.stack([factor * jnp.cos(phases), -factor * jnp.sin(phases)], axis=4)
    return twiddle.reshape(STEPS_T, GRID_Z, 2 * MODES_T * MODES_Z).astype(jnp.bfloat16)


def line_parts(kept_count, axis_length):
    frequency = kept_modes(kept_count, axis_length)
    positions = jnp.arange(axis_length, dtype=jnp.int32)
    phase_index = frequency[:, None] * positions[None, :] % axis_length
    phases = 2.0 * math.pi / axis_length * phase_index.astype(jnp.float32)
    factor = 1.0 / math.sqrt(axis_length)
    return factor * jnp.cos(phases), factor * jnp.sin(phases)


def line_matrix(kept_count, axis_length):
    frequency = kept_modes(kept_count, axis_length)
    positions = jnp.arange(axis_length, dtype=jnp.int32)
    phase_index = frequency[:, None] * positions[None, :] % axis_length
    phases = 2.0 * math.pi / axis_length * phase_index.astype(jnp.float32)
    factor = 1.0 / math.sqrt(axis_length)
    cosines = factor * jnp.cos(phases)
    sines = factor * jnp.sin(phases)
    upper = jnp.stack([cosines, sines], axis=1)
    lower = jnp.stack([-sines, cosines], axis=1)
    return jnp.stack([upper, lower], axis=0)


def plane_table_fast():
    moments = jnp.arange(STEPS_T, dtype=jnp.int32)
    depths = jnp.arange(GRID_Z, dtype=jnp.int32)
    time_freq = jnp.arange(MODES_T, dtype=jnp.int32)
    depth_freq = kept_modes(MODES_Z, GRID_Z)
    step = 2.0 * math.pi / GRID_Z
    time_phase = step * ((moments[:, None] * time_freq[None, :] * (GRID_Z // STEPS_T)) % GRID_Z).astype(jnp.float32)
    depth_phase = step * ((depths[:, None] * depth_freq[None, :]) % GRID_Z).astype(jnp.float32)
    factor = 1.0 / math.sqrt(STEPS_T * GRID_Z)
    ct = (factor * jnp.cos(time_phase))[:, None, :, None]
    st = (factor * jnp.sin(time_phase))[:, None, :, None]
    cz = jnp.cos(depth_phase)[None, :, None, :]
    sz = jnp.sin(depth_phase)[None, :, None, :]
    cos_part = ct * cz - st * sz
    sin_part = st * cz + ct * sz
    twiddle = jnp.stack([cos_part.reshape(STEPS_T, GRID_Z, MODES_T, 2, HALF_Z),
                         -sin_part.reshape(STEPS_T, GRID_Z, MODES_T, 2, HALF_Z)], axis=4)
    return twiddle.reshape(STEPS_T, GRID_Z, 2 * MODES_T * MODES_Z).astype(jnp.bfloat16)


def one_sample(moved, mode_weights, kron, second):
    high = lax.Precision.HIGH
    pairs, parts_x, _, lanes = moved.shape
    parts_y = second.shape[0]
    rows_y = second.shape[1] // 2
    kept_here = MODES_X // parts_y

    moved = moved.reshape(pairs, parts_x * 2, HALF_Z, lanes)
    upper = moved.astype(jnp.bfloat16)
    lower = (moved - upper.astype(jnp.float32)).astype(jnp.bfloat16)
    numbers = (((1, 2), (1, 3)), ((), ()))
    kron_upper, kron_lower = kron
    after_x = (
        lax.dot_general(kron_upper, upper, numbers, preferred_element_type=jnp.float32)
        + lax.dot_general(kron_upper, lower, numbers, preferred_element_type=jnp.float32)
        + lax.dot_general(kron_lower, upper, numbers, preferred_element_type=jnp.float32)
    )
    after_x = after_x.reshape(parts_y, kept_here * 2 * rows_y, pairs * HALF_Z)
    gathered = lax.all_to_all(after_x, "gy", 0, 0, tiled=False)
    gathered = gathered.reshape(parts_y, kept_here, 2 * rows_y, pairs * HALF_Z)

    numbers = (((0, 2), (0, 1)), ((1,), (2,)))
    upper = gathered.astype(jnp.bfloat16)
    lower = (gathered - upper.astype(jnp.float32)).astype(jnp.bfloat16)
    second_upper = second.astype(jnp.bfloat16)
    second_lower = (second - second_upper.astype(jnp.float32)).astype(jnp.bfloat16)
    after_y = (
        lax.dot_general(upper, second_upper, numbers, preferred_element_type=jnp.float32)
        + lax.dot_general(lower, second_upper, numbers, preferred_element_type=jnp.float32)
        + lax.dot_general(upper, second_lower, numbers, preferred_element_type=jnp.float32)
    )
    after_y = after_y.reshape(kept_here, pairs, HALF_Z, 2, MODES_Y)
    after_y = jnp.transpose(after_y, (0, 1, 3, 2, 4))
    after_y = after_y.reshape(kept_here, pairs, 2, HALF_Z * MODES_Y)

    real_part = after_y[:, :, None, 0]
    imag_part = after_y[:, :, None, 1]
    weight_re = mode_weights[:, :, :, 0, 0].astype(jnp.float32)
    weight_im = mode_weights[:, :, :, 0, 1].astype(jnp.float32)
    mixed_re = jnp.sum(real_part * weight_re - imag_part * weight_im, axis=1)
    mixed_im = jnp.sum(real_part * weight_im + imag_part * weight_re, axis=1)
    return jnp.stack([mixed_re, mixed_im], axis=2)[:, :, None]


def local(plume_field, mode_weights):
    samples, channels, rows_x, rows_y = plume_field.shape[:4]
    parts_x = GRID_X // rows_x
    parts_y = GRID_Y // rows_y
    groups = 2 * MODES_T
    per_group = 2 * HALF_Z
    kept_here = MODES_X // parts_y
    lanes = rows_x * rows_y
    pairs = samples * channels

    twiddle = plane_table_fast()
    field = plume_field.reshape(pairs, lanes, STEPS_T, GRID_Z)
    spectrum = jnp.einsum("tzn,Bxtz->Bnx", twiddle, field, preferred_element_type=jnp.float32)
    spectrum = spectrum.reshape(samples, channels, groups, per_group, lanes)

    second = line_matrix(MODES_Y, GRID_Y).reshape(2, MODES_Y, 2, parts_y, rows_y)
    second = jnp.transpose(second, (3, 2, 4, 0, 1)).reshape(parts_y, 2 * rows_y, 1, 2 * MODES_Y)
    second = jnp.broadcast_to(second, (parts_y, 2 * rows_y, kept_here, 2 * MODES_Y))

    chunks = [spectrum[sample] for sample in range(samples)]
    first = line_matrix(MODES_X, GRID_X).reshape(2, parts_y, kept_here, 2, parts_x, rows_x)
    outs = []
    for sample in range(samples):
        moved = lax.all_to_all(chunks[sample], "gx", 1, 1, tiled=False)
        if sample == 0:
            first, moved = lax.optimization_barrier((first, moved))
            first = jnp.transpose(first, (1, 2, 0, 4, 3, 5)).reshape(MODES_X * 2, parts_x * 2, rows_x)
            lane = jnp.arange(lanes, dtype=jnp.int32)
            spread = (lane[None, :] // rows_y == jnp.arange(rows_x, dtype=jnp.int32)[:, None]).astype(jnp.float32)
            keep = (lane[None, :] % rows_y == jnp.arange(rows_y, dtype=jnp.int32)[:, None]).astype(jnp.float32)
            spread_first = jnp.einsum("aip,pq->aiq", first, spread, precision=lax.Precision.HIGHEST)
            kron = spread_first[:, None] * keep[None, :, None, :]
            kron = kron.reshape(MODES_X * 2 * rows_y, parts_x * 2, lanes)
            kron_upper = kron.astype(jnp.bfloat16)
            kron = (kron_upper, (kron - kron_upper.astype(jnp.float32)).astype(jnp.bfloat16))
        outs.append(one_sample(moved, mode_weights, kron, second))
    return jnp.stack(outs, axis=0)


def solution(mesh):
    return jax.shard_map(
        local,
        mesh=mesh,
        in_specs=(P(None, None, "gx", "gy", None, None), P("gy", None, None, "gx", None, None)),
        out_specs=P(None, "gy", None, "gx", None, None),
        check_vma=False,
    )
```

```python
import math

import jax
import jax.numpy as jnp
from jax import lax
from jax.sharding import PartitionSpec as P

GRID_X = 128
GRID_Y = 128
GRID_Z = 128
STEPS_T = 16
MODES_X = 24
MODES_Y = 24
MODES_Z = 24
MODES_T = 8
HALF_Z = 12


def kept_modes(kept_count, axis_length):
    position = jnp.arange(kept_count, dtype=jnp.int32)
    return jnp.where(position < kept_count // 2, position, axis_length - kept_count + position)


def plane_table():
    moments = jnp.arange(STEPS_T, dtype=jnp.int32)
    depths = jnp.arange(GRID_Z, dtype=jnp.int32)
    time_freq = jnp.arange(MODES_T, dtype=jnp.int32)
    depth_freq = kept_modes(MODES_Z, GRID_Z).reshape(2, HALF_Z)
    phase_index = (
        time_freq[None, None, :, None, None]
        * moments[:, None, None, None, None]
        * (GRID_Z // STEPS_T)
        + depth_freq[None, None, None, :, :] * depths[None, :, None, None, None]
    ) % GRID_Z
    phases = 2.0 * math.pi / GRID_Z * phase_index.astype(jnp.float32)
    factor = 1.0 / math.sqrt(STEPS_T * GRID_Z)
    twiddle = jnp.stack([factor * jnp.cos(phases), -factor * jnp.sin(phases)], axis=4)
    return twiddle.reshape(STEPS_T, GRID_Z, 2 * MODES_T * MODES_Z).astype(jnp.bfloat16)


def line_parts(kept_count, axis_length):
    frequency = kept_modes(kept_count, axis_length)
    positions = jnp.arange(axis_length, dtype=jnp.int32)
    phase_index = frequency[:, None] * positions[None, :] % axis_length
    phases = 2.0 * math.pi / axis_length * phase_index.astype(jnp.float32)
    factor = 1.0 / math.sqrt(axis_length)
    return factor * jnp.cos(phases), factor * jnp.sin(phases)


def line_matrix(kept_count, axis_length):
    frequency = kept_modes(kept_count, axis_length)
    positions = jnp.arange(axis_length, dtype=jnp.int32)
    phase_index = frequency[:, None] * positions[None, :] % axis_length
    phases = 2.0 * math.pi / axis_length * phase_index.astype(jnp.float32)
    factor = 1.0 / math.sqrt(axis_length)
    cosines = factor * jnp.cos(phases)
    sines = factor * jnp.sin(phases)
    upper = jnp.stack([cosines, sines], axis=1)
    lower = jnp.stack([-sines, cosines], axis=1)
    return jnp.stack([upper, lower], axis=0)


def plane_table_fast():
    moments = jnp.arange(STEPS_T, dtype=jnp.int32)
    depths = jnp.arange(GRID_Z, dtype=jnp.int32)
    time_freq = jnp.arange(MODES_T, dtype=jnp.int32)
    depth_freq = kept_modes(MODES_Z, GRID_Z)
    step = 2.0 * math.pi / GRID_Z
    time_phase = step * ((moments[:, None] * time_freq[None, :] * (GRID_Z // STEPS_T)) % GRID_Z).astype(jnp.float32)
    depth_phase = step * ((depths[:, None] * depth_freq[None, :]) % GRID_Z).astype(jnp.float32)
    factor = 1.0 / math.sqrt(STEPS_T * GRID_Z)
    ct = (factor * jnp.cos(time_phase))[:, None, :, None]
    st = (factor * jnp.sin(time_phase))[:, None, :, None]
    cz = jnp.cos(depth_phase)[None, :, None, :]
    sz = jnp.sin(depth_phase)[None, :, None, :]
    cos_part = ct * cz - st * sz
    sin_part = st * cz + ct * sz
    twiddle = jnp.stack([cos_part.reshape(STEPS_T, GRID_Z, MODES_T, 2, HALF_Z),
                         -sin_part.reshape(STEPS_T, GRID_Z, MODES_T, 2, HALF_Z)], axis=4)
    return twiddle.reshape(STEPS_T, GRID_Z, 2 * MODES_T * MODES_Z).astype(jnp.bfloat16)


def one_sample(moved, mode_weights, kron, second):
    high = lax.Precision.HIGH
    pairs, parts_x, _, lanes = moved.shape
    parts_y = second.shape[0]
    rows_y = second.shape[1] // 2
    kept_here = MODES_X // parts_y

    moved = moved.reshape(pairs, parts_x * 2, HALF_Z, lanes)
    upper = moved.astype(jnp.bfloat16)
    lower = (moved - upper.astype(jnp.float32)).astype(jnp.bfloat16)
    numbers = (((1, 2), (1, 3)), ((), ()))
    kron_upper, kron_lower = kron
    after_x = (
        lax.dot_general(kron_upper, upper, numbers, preferred_element_type=jnp.float32)
        + lax.dot_general(kron_upper, lower, numbers, preferred_element_type=jnp.float32)
        + lax.dot_general(kron_lower, upper, numbers, preferred_element_type=jnp.float32)
    )
    after_x = after_x.reshape(parts_y, kept_here * 2 * rows_y, pairs * HALF_Z)
    gathered = lax.all_to_all(after_x, "gy", 0, 0, tiled=False)
    gathered = gathered.reshape(parts_y, kept_here, 2 * rows_y, pairs * HALF_Z)

    after_y = lax.dot_general(gathered, second, (((0, 2), (0, 1)), ((1,), (2,))), precision=high)
    after_y = after_y.reshape(kept_here, pairs, HALF_Z, 2, MODES_Y)
    after_y = jnp.transpose(after_y, (0, 1, 3, 2, 4))
    after_y = after_y.reshape(kept_here, pairs, 2, HALF_Z * MODES_Y)

    real_part = after_y[:, :, None, 0]
    imag_part = after_y[:, :, None, 1]
    weight_re = mode_weights[:, :, :, 0, 0].astype(jnp.float32)
    weight_im = mode_weights[:, :, :, 0, 1].astype(jnp.float32)
    mixed_re = jnp.sum(real_part * weight_re - imag_part * weight_im, axis=1)
    mixed_im = jnp.sum(real_part * weight_im + imag_part * weight_re, axis=1)
    return jnp.stack([mixed_re, mixed_im], axis=2)[:, :, None]


def local(plume_field, mode_weights):
    samples, channels, rows_x, rows_y = plume_field.shape[:4]
    parts_x = GRID_X // rows_x
    parts_y = GRID_Y // rows_y
    groups = 2 * MODES_T
    per_group = 2 * HALF_Z
    kept_here = MODES_X // parts_y
    lanes = rows_x * rows_y
    pairs = samples * channels

    twiddle = plane_table_fast()
    field = plume_field.reshape(pairs, lanes, STEPS_T, GRID_Z)
    twiddle = twiddle.reshape(STEPS_T, GRID_Z, groups, per_group)
    spectrum = jnp.einsum("tzgr,Bxtz->gBrx", twiddle, field, preferred_element_type=jnp.float32)
    spectrum = spectrum.reshape(groups, samples, channels, per_group, lanes)

    second = line_matrix(MODES_Y, GRID_Y).reshape(2, MODES_Y, 2, parts_y, rows_y)
    second = jnp.transpose(second, (3, 2, 4, 0, 1)).reshape(parts_y, 2 * rows_y, 1, 2 * MODES_Y)
    second = jnp.broadcast_to(second, (parts_y, 2 * rows_y, kept_here, 2 * MODES_Y))

    chunks = [spectrum[:, sample] for sample in range(samples)]
    first = line_matrix(MODES_X, GRID_X).reshape(2, parts_y, kept_here, 2, parts_x, rows_x)
    outs = []
    for sample in range(samples):
        moved = lax.all_to_all(chunks[sample], "gx", 0, 1, tiled=False)
        if sample == 0:
            first, moved = lax.optimization_barrier((first, moved))
            first = jnp.transpose(first, (1, 2, 0, 4, 3, 5)).reshape(MODES_X * 2, parts_x * 2, rows_x)
            lane = jnp.arange(lanes, dtype=jnp.int32)
            spread = (lane[None, :] // rows_y == jnp.arange(rows_x, dtype=jnp.int32)[:, None]).astype(jnp.float32)
            keep = (lane[None, :] % rows_y == jnp.arange(rows_y, dtype=jnp.int32)[:, None]).astype(jnp.float32)
            spread_first = jnp.einsum("aip,pq->aiq", first, spread, precision=lax.Precision.HIGHEST)
            kron = spread_first[:, None] * keep[None, :, None, :]
            kron = kron.reshape(MODES_X * 2 * rows_y, parts_x * 2, lanes)
            kron_upper = kron.astype(jnp.bfloat16)
            kron = (kron_upper, (kron - kron_upper.astype(jnp.float32)).astype(jnp.bfloat16))
        outs.append(one_sample(moved, mode_weights, kron, second))
    return jnp.stack(outs, axis=0)


def solution(mesh):
    return jax.shard_map(
        local,
        mesh=mesh,
        in_specs=(P(None, None, "gx", "gy", None, None), P("gy", None, None, "gx", None, None)),
        out_specs=P(None, "gy", None, "gx", None, None),
        check_vma=False,
    )
```
